128 devices in a mesh: req: 8 (over z, core), seq: 16 (over x, y).
Axes of the slice: x: 4, y: 4, z: 4, core: 2. Of those that a mesh axis runs over, the one named last changes fastest.
Arguments:
- token_ids: int32 [64, 4], replicated, may hold values from 0 to 127999, as said below
- embed_table: bfloat16 [128000, 1024], P(('req', 'seq')), may hold values from -6 to 6
- ln_gains: float32 [4, 1024], replicated, may hold values from 0.25 to 1.75
- ln_biases: float32 [4, 1024], replicated, may hold values from -1.5 to 1.5
- rel_table: bfloat16 [512, 1024], replicated, may hold values from -6 to 6
- w_qkv: bfloat16 [1024, 3072], replicated, may hold values from -0.1875 to 0.1875
- w_out: bfloat16 [1024, 1024], replicated, may hold values from -0.1875 to 0.1875
- cache_keys: bfloat16 [64, 8192, 1024], P('req', 'seq'), may hold values from -3000 to 3000
- cache_values: bfloat16 [64, 8192, 1024], P('req', 'seq'), may hold values from -6 to 6
- lengths: int32 [64], P('req'), may hold values from 129 to 8192, as said below
- window_starts: int32 [64], P('req'), may hold values from 4 to 4096, as said below
- cache_buckets: int32 [64, 4, 8192], P('req', None, 'seq'), may hold values from 0 to 511
- new_buckets: int32 [64, 4, 4], P('req'), may hold values from 0 to 511
- w_in: bfloat16 [4096, 1024], P('seq'), may hold values from -0.1875 to 0.1875
- w_down: bfloat16 [4096, 1024], P('seq'), may hold values from -0.09375 to 0.09375
Outputs:
- layer_out: bfloat16 [64, 4, 1024], P('req')
The draws below stay inside these ranges and needn't reach their ends.
Inputs may be any that keep to these rules, and one draw needn't show every extreme that they name: `token_ids`: every aligned block of 1000 ids holds the id of at least one new token. `lengths`: some request has length 8192. window_starts = max(4, lengths - 4096) for each request.
All inputs are finite; a program needn't handle non-finite values.
Results may differ from the reference program's by a relative error of at most 0.018.
Values may be sent and summed in bfloat16 or wider, within the bound.
A program may use at most 192 MiB of HBM per device.

```python
import math
import jax
import jax.numpy as jnp
from jax import lax

D = 1024
HEADS = 16
FF = 4096
BUCKETS = 512
HEAD_DIM = 64
VOCAB_DEV = 1000
VOCAB = 128000
REQS = 64
NEW = 4
CACHE = 8192
SINKS = 4
WINDOW = 4096


def length_draw(key):
    base_key = jax.random.fold_in(key, 11)
    first_key, second_key, third_key, fourth_key = jax.random.split(base_key, 4)
    shifts = jax.random.randint(first_key, (REQS,), 0, 6)
    base_len = CACHE // jnp.power(2, shifts)
    cut_len = jax.random.randint(second_key, (REQS,), 0, base_len // 2)
    chosen = jax.random.randint(third_key, (), 0, REQS)
    other = (chosen + 1 + jax.random.randint(fourth_key, (), 0, REQS - 1)) % REQS
    rows = jnp.arange(REQS)
    picked = jnp.where(rows == chosen, CACHE, base_len - cut_len)
    picked = jnp.where(rows == other, CACHE // 64 + 1, picked)
    return picked.astype(jnp.int32)


def draw_lengths(key, part):
    return length_draw(key)


def draw_window_starts(key, part):
    return jnp.maximum(length_draw(key) - WINDOW, SINKS).astype(jnp.int32)


def draw_token_ids(key, part):
    first_key, second_key = jax.random.split(jax.random.fold_in(key, 31))
    total_ids = REQS * NEW
    owners = VOCAB // VOCAB_DEV
    order = jax.random.permutation(first_key, total_ids)
    offsets = jax.random.randint(second_key, (total_ids,), 0, VOCAB_DEV)
    return (order % owners * VOCAB_DEV + offsets).reshape(REQS, NEW).astype(jnp.int32)


def draw_cache_keys(key, part):
    first_key = jax.random.fold_in(jax.random.fold_in(key, 41), 0)
    values = jnp.clip(jax.random.normal(first_key, (REQS, CACHE, D), jnp.float32), -6.0, 6.0)
    return values.astype(jnp.bfloat16)


def place_ends(entries, rng, least, high):
    shape = entries.shape
    spot = [jax.random.randint(jax.random.fold_in(rng, axis), (), 0, shape[axis]) for axis in range(len(shape))]
    entries = entries.at[tuple(spot)].set(least)
    longest = shape.index(max(shape))
    spot[longest] = (spot[longest] + 1) % shape[longest]
    return entries.at[tuple(spot)].set(high)


def block_levels(key, shape, cuts, smallest, top_value):
    factor_of, own = 1.0, jax.random.fold_in(key, 6)
    for dim, shards_of in cuts:
        steps = jnp.exp(jax.random.uniform(jax.random.fold_in(own, dim), (shards_of,), jnp.float32, smallest / len(cuts), top_value / len(cuts)))
        factor_of = factor_of * jnp.repeat(steps, shape[dim] // shards_of).reshape([-1 if axis == dim else 1 for axis in range(len(shape))])
    return factor_of


def scatter_about(rng, shape, scale, bound, shards=(), held_as=jnp.bfloat16):
    values = jax.random.normal(rng, shape, jnp.float32) * scale
    if len(shards) > 0:
        values = block_levels(rng, shape, shards, -0.22, 0.18) * values
    return jnp.clip(values, min=-bound, max=bound).astype(held_as)


def setup_inputs(seed: int = 0) -> dict:
    key_of = jax.random.split(jax.random.key(seed), 16)
    return {
        "token_ids": draw_token_ids(jax.random.fold_in(key_of[15], 71), 0),
        "embed_table": scatter_about(key_of[1], (VOCAB, D), 1.0, 6.0, ((0, 128),)),
        "ln_gains": jnp.clip(1.0 + 0.15 * jax.random.normal(key_of[2], (4, D), jnp.float32), 0.25, 1.75),
        "ln_biases": scatter_about(key_of[3], (4, D), 0.3, 1.5, (), jnp.float32),
        "rel_table": scatter_about(key_of[4], (BUCKETS, D), 1.0, 6.0),
        "w_qkv": scatter_about(key_of[5], (D, 3 * D), D ** -0.5, 0.1875),
        "w_out": scatter_about(key_of[6], (D, D), D ** -0.5, 0.1875),
        "cache_keys": draw_cache_keys(jax.random.fold_in(key_of[15], 71), 0),
        "cache_values": scatter_about(key_of[8], (REQS, CACHE, D), 1.0, 6.0, ((0, 8), (1, 16))),
        "lengths": draw_lengths(jax.random.fold_in(key_of[15], 71), 0),
        "window_starts": draw_window_starts(jax.random.fold_in(key_of[15], 71), 0),
        "cache_buckets": place_ends(jax.random.randint(key_of[11], (REQS, NEW, CACHE), 0, BUCKETS), jax.random.fold_in(key_of[11], 1), 0, BUCKETS - 1).astype(jnp.int32),
        "new_buckets": place_ends(jax.random.randint(key_of[12], (REQS, NEW, NEW), 0, BUCKETS), jax.random.fold_in(key_of[12], 1), 0, BUCKETS - 1).astype(jnp.int32),
        "w_in": scatter_about(key_of[13], (FF, D), D ** -0.5, 0.1875, ((0, 16),)),
        "w_down": scatter_about(key_of[14], (FF, D), FF ** -0.5, 0.09375, ((0, 16),)),
    }


norm_epsilon = 1e-06
masked_score = -1e+30

def layer_norm(values, gain, shift):
    center = values - lax.optimization_barrier(jnp.mean(values, axis=-1, keepdims=True))
    spread = lax.optimization_barrier(jnp.mean(center * center, axis=-1, keepdims=True))
    return center * lax.rsqrt(spread + norm_epsilon) * gain + shift

def reference(token_ids, embed_table, ln_gains, ln_biases, rel_table, w_qkv, w_out, cache_keys, cache_values, lengths, window_starts, cache_buckets, new_buckets, w_in, w_down):
    looked_up = jnp.take(embed_table, token_ids.reshape(-1), axis=0).astype(jnp.float32)
    hidden_zero = layer_norm(looked_up, ln_gains[0], ln_biases[0]).astype(jnp.bfloat16)
    relative = layer_norm(rel_table.astype(jnp.float32), ln_gains[3], ln_biases[3]).astype(jnp.bfloat16)
    pos_query = jnp.dot(relative, w_qkv[:, :D], preferred_element_type=jnp.float32).astype(jnp.bfloat16)
    pos_key = jnp.dot(relative, w_qkv[:, D:2 * D], preferred_element_type=jnp.float32).astype(jnp.bfloat16)
    projected = jnp.dot(hidden_zero, w_qkv, preferred_element_type=jnp.float32).astype(jnp.bfloat16)
    projected = projected.reshape(REQS, NEW, 3, HEADS, HEAD_DIM)
    score_scale = 1.0 / math.sqrt(3 * HEAD_DIM)
    pos_key_heads = pos_key.astype(jnp.float32).reshape(BUCKETS, HEADS, HEAD_DIM)
    total_len = CACHE + NEW
    places = jnp.arange(total_len, dtype=jnp.int32)
    fresh_live = (places[None, :] >= CACHE) & (places[None, :] - CACHE <= jnp.arange(NEW, dtype=jnp.int32)[:, None])

    def one_request(items):
        queries, fresh_keys, fresh_values, old_keys, old_values, length, start, old_buckets, fresh_buckets = items
        key_rows = jnp.concatenate([old_keys, fresh_keys.reshape(NEW, D)], axis=0).astype(jnp.float32).reshape(total_len, HEADS, HEAD_DIM)
        value_rows = jnp.concatenate([old_values, fresh_values.reshape(NEW, D)], axis=0).astype(jnp.float32).reshape(total_len, HEADS, HEAD_DIM)
        bucket_rows = jnp.concatenate([old_buckets, fresh_buckets], axis=1).astype(jnp.int32)
        query_float = queries.astype(jnp.float32)
        content = jnp.einsum('thd,lhd->htl', query_float, key_rows)
        table = jnp.einsum('thd,bhd->htb', query_float, pos_key_heads)
        to_pos = jnp.take_along_axis(table, jnp.broadcast_to(bucket_rows[None], (HEADS, NEW, total_len)), axis=2)
        gathered = jnp.take(pos_query, BUCKETS - 1 - bucket_rows, axis=0).astype(jnp.float32).reshape(NEW, total_len, HEADS, HEAD_DIM)
        from_pos = jnp.einsum('tlhd,lhd->htl', gathered, key_rows)
        cache_live = (places < length) & ((places < SINKS) | (places >= start)) & (places < CACHE)
        allowed = cache_live[None, :] | fresh_live
        scores = jnp.where(allowed[None], (content + to_pos + from_pos) * score_scale, masked_score)
        row_max = lax.optimization_barrier(jnp.max(scores, axis=-1, keepdims=True))
        exp_terms = jnp.where(allowed[None], jnp.exp(scores - row_max), 0.0)
        exp_rounded = lax.optimization_barrier(exp_terms.astype(jnp.bfloat16)).astype(jnp.float32)
        numerator = jnp.einsum('htl,lhd->thd', exp_rounded, value_rows)
        denominator = lax.optimization_barrier(jnp.sum(exp_terms, axis=-1))
        return (numerator / jnp.transpose(denominator)[:, :, None]).astype(jnp.bfloat16).reshape(NEW, D)
    attended = lax.map(one_request, (projected[:, :, 0], projected[:, :, 1], projected[:, :, 2], cache_keys, cache_values, lengths, window_starts, cache_buckets, new_buckets))
    attn_out = jnp.dot(attended.reshape(REQS * NEW, D), w_out, preferred_element_type=jnp.float32)
    hidden_one = layer_norm(hidden_zero.astype(jnp.float32) + attn_out, ln_gains[1], ln_biases[1]).astype(jnp.bfloat16)
    inner = jax.nn.gelu(jnp.dot(hidden_one, jnp.transpose(w_in), preferred_element_type=jnp.float32), approximate=False).astype(jnp.bfloat16)
    mlp_out = jnp.dot(inner, w_down, preferred_element_type=jnp.float32)
    layer_out = layer_norm(hidden_one.astype(jnp.float32) + mlp_out, ln_gains[2], ln_biases[2]).astype(jnp.bfloat16)
    return layer_out.reshape(REQS, NEW, D)
```

```python
import functools
import math

import jax
import jax.numpy as jnp
from jax import lax
from jax.experimental import pallas as pl
from jax.experimental.pallas import tpu as pltpu
from jax.sharding import PartitionSpec as P

HEADS = 16
HEAD_DIM = 64
SINKS = 4
NEW = 4
WIDTH = 1024
REQ_N = 8
SEQ_N = 16
GROUP = 8
ROWS = GROUP * NEW
PIECE = 512
BUCKETS = 512
TILE = 256
LANES = 128
CHUNKS = WIDTH // LANES
MSG = 24

norm_epsilon = 1e-06
masked_score = -1e30
score_scale = 1.0 / math.sqrt(3 * HEAD_DIM)
MESH = pl.DeviceIdType.MESH
f32 = jnp.float32
bf16 = jnp.bfloat16


def layer_norm(values, gain, shift):
    center = values - jnp.mean(values, axis=-1, keepdims=True)
    spread = jnp.mean(center * center, axis=-1, keepdims=True)
    return center * lax.rsqrt(spread + norm_epsilon) * gain + shift


def dot_nt(a, b):
    return lax.dot_general(a, b, (((1,), (1,)), ((), ())), preferred_element_type=f32)


def rows_to_tiles(rows, stage, count):
    for c in range(CHUNKS):
        stage[pl.ds(c, count, stride=CHUNKS), :] = rows[:, c * LANES : (c + 1) * LANES]


def tiles_to_rows(stage, count):
    return jnp.concatenate(
        [stage[pl.ds(c, count, stride=CHUNKS), :] for c in range(CHUNKS)], axis=1
    )


def seq_copy(src, dst, send_sem, recv_sem, peer):
    return pltpu.make_async_remote_copy(
        src_ref=src,
        dst_ref=dst,
        send_sem=send_sem,
        recv_sem=recv_sem,
        device_id={"seq": peer},
        device_id_type=MESH,
    )


def seq_scatter(me, send, recv, send_sems, recv_sems):
    copies = []
    for k in range(1, SEQ_N):
        peer = lax.rem(me + k, SEQ_N)
        copy = seq_copy(send.at[peer], recv.at[k], send_sems.at[k], recv_sems.at[k], peer)
        copy.start()
        copies.append(copy)
    return copies


def seq_gather(me, buf, send_sems, recv_sems):
    copies = []
    for k in range(1, SEQ_N):
        peer = lax.rem(me + k, SEQ_N)
        copy = seq_copy(buf.at[me], buf.at[me], send_sems.at[k], recv_sems.at[k], peer)
        copy.start()
        copies.append(copy)
    return copies


def wait_all(copies):
    for copy in copies:
        copy.wait()


def embed_kernel(
    ids_ref, table_ref, gain_ref, bias_ref, out_ref, send, land, stage, tiles, got, hid, rows_f,
    req_send, req_recv, rs_send, rs_recv, ag_send, ag_recv,
):
    me = lax.axis_index("seq")
    req = lax.axis_index("req")
    barrier = pltpu.get_barrier_semaphore()
    for k in range(1, SEQ_N):
        pl.semaphore_signal(
            barrier, inc=1, device_id={"seq": lax.rem(me + k, SEQ_N)}, device_id_type=MESH
        )
    for k in range(1, REQ_N):
        pl.semaphore_signal(
            barrier, inc=1, device_id={"req": lax.rem(req + k, REQ_N)}, device_id_type=MESH
        )
    vocab_rows = table_ref.shape[0]
    local = ids_ref[...] - (req * SEQ_N + me) * vocab_rows
    one_hot = (
        lax.broadcasted_iota(jnp.int32, (REQ_N * ROWS, vocab_rows), 1) == local
    ).astype(f32).astype(bf16)
    send[...] = (
        jnp.dot(one_hot, table_ref[...], preferred_element_type=f32)
        .astype(bf16)
        .reshape(REQ_N, ROWS, WIDTH)
    )
    pl.semaphore_wait(barrier, SEQ_N - 1 + REQ_N - 1)
    copies = []
    for k in range(1, REQ_N):
        peer = lax.rem(req + k, REQ_N)
        copy = pltpu.make_async_remote_copy(
            src_ref=send.at[peer],
            dst_ref=land.at[k],
            send_sem=req_send.at[k],
            recv_sem=req_recv.at[k],
            device_id={"req": peer},
            device_id_type=MESH,
        )
        copy.start()
        copies.append(copy)
    total = send[req].astype(f32)
    for k in range(1, REQ_N):
        copies[k - 1].wait()
        total = total + land[k].astype(f32)
    rows_to_tiles(total, stage, ROWS)
    tiles[...] = stage[...].reshape(SEQ_N, 2 * CHUNKS, LANES).astype(bf16)
    copies = seq_scatter(me, tiles, got, rs_send, rs_recv)
    own = tiles[me].astype(f32)
    for k in range(1, SEQ_N):
        copies[k - 1].wait()
        own = own + got[k].astype(f32)
    rows_f[...] = own
    hidden = layer_norm(tiles_to_rows(rows_f, 2), gain_ref[0:1, :], bias_ref[0:1, :])
    rows_to_tiles(hidden, rows_f, 2)
    hid[me] = rows_f[...].astype(bf16)
    wait_all(seq_gather(me, hid, ag_send, ag_recv))
    stage[...] = hid[...].astype(f32).reshape(ROWS * CHUNKS, LANES)
    out_ref[...] = tiles_to_rows(stage, ROWS).astype(bf16)


def embed_call(ids, table, gains, biases):
    slot = (SEQ_N, 2 * CHUNKS, LANES)
    return pl.pallas_call(
        embed_kernel,
        out_shape=jax.ShapeDtypeStruct((ROWS, WIDTH), bf16),
        in_specs=[pl.BlockSpec(memory_space=pltpu.VMEM)] * 4,
        out_specs=pl.BlockSpec(memory_space=pltpu.VMEM),
        scratch_shapes=[
            pltpu.VMEM((REQ_N, ROWS, WIDTH), bf16),
            pltpu.VMEM((REQ_N, ROWS, WIDTH), bf16),
            pltpu.VMEM((ROWS * CHUNKS, LANES), f32),
            pltpu.VMEM(slot, bf16),
            pltpu.VMEM(slot, bf16),
            pltpu.VMEM(slot, bf16),
            pltpu.VMEM((2 * CHUNKS, LANES), f32),
        ]
        + [pltpu.SemaphoreType.DMA((REQ_N,))] * 2
        + [pltpu.SemaphoreType.DMA((SEQ_N,))] * 4,
        compiler_params=pltpu.CompilerParams(
            collective_id=0, has_side_effects=True, vmem_limit_bytes=32 << 20
        ),
        name="embed_exchange",
    )(ids, table, gains, biases)


def spread_pair(column_even, column_odd, lane):
    return jnp.where(lane < HEAD_DIM, column_even, column_odd)


def pack_ml(values, lane):
    out = jnp.zeros((CHUNKS, LANES), f32)
    for g, value in enumerate(values):
        out = jnp.where((lane >> 4) == g, value, out)
    return out


def attend_kernel(
    lengths_ref, starts_ref, place_ref,
    hidden_ref, rel_ref, gain_ref, bias_ref, w_ref, keys_ref, values_ref, buckets_ref, new_ref,
    msg_ref, fresh_ref,
    proj, pos_lhs, pos_key, keys_t, from_pos, stage, fresh_stage,
):
    r = pl.program_id(0)
    lane = lax.broadcasted_iota(jnp.int32, (CHUNKS, LANES), 1)
    table_rows = NEW * HEADS

    @pl.when(r == 0)
    def _():
        relative = layer_norm(rel_ref[...].astype(f32), gain_ref[3:4, :], bias_ref[3:4, :]).astype(
            bf16
        )
        flip = (
            lax.broadcasted_iota(jnp.int32, (BUCKETS, BUCKETS), 0)
            + lax.broadcasted_iota(jnp.int32, (BUCKETS, BUCKETS), 1)
            == BUCKETS - 1
        ).astype(f32).astype(bf16)
        flipped = jnp.dot(flip, relative, preferred_element_type=f32).astype(bf16)
        pos_lhs[0:WIDTH, :] = (
            jnp.dot(flipped, w_ref[:, 0:WIDTH], preferred_element_type=f32).astype(bf16).T
        )
        pos_key[...] = jnp.dot(
            relative, w_ref[:, WIDTH : 2 * WIDTH], preferred_element_type=f32
        ).astype(bf16)
        projected = (
            jnp.dot(hidden_ref[...], w_ref[...], preferred_element_type=f32)
            .astype(bf16)
            .astype(f32)
        )
        for one in range(GROUP):
            proj[one] = projected[one * NEW : (one + 1) * NEW, :]

    length = lengths_ref[r]
    start = starts_ref[r]
    first = place_ref[0] * PIECE
    live = (first < length) & ((first < SINKS) | (first + PIECE > start))

    @pl.when(jnp.logical_not(live))
    def _():
        parts = lax.broadcasted_iota(jnp.int32, (2, MSG, LANES), 1)
        lanes = lax.broadcasted_iota(jnp.int32, (2, MSG, LANES), 2)
        msg_ref[...] = jnp.where(
            (parts >= 2 * CHUNKS) & ((lanes & 16) == 0), masked_score, 0.0
        )

    @pl.when(live)
    def _():
        keys = keys_ref[...]
        keys_t[...] = keys.T.astype(f32)
        q4 = proj[r, :, 0:WIDTH]
        q_all = jnp.broadcast_to(q4[:, None, :], (NEW, HEADS, WIDTH))
        row = lax.broadcasted_iota(jnp.int32, (NEW, HEADS, WIDTH), 1)
        col_head = lax.broadcasted_iota(jnp.int32, (NEW, HEADS, WIDTH), 2) >> 6
        row_head = 2 * (row & (CHUNKS - 1)) + (row >> 3)
        own_head = row_head == col_head
        queries = (
            jnp.where(own_head, q_all, 0.0).reshape(table_rows, WIDTH).astype(bf16)
        )
        content = dot_nt(queries, keys)
        to_table = dot_nt(queries, pos_key[...])
        high = to_table.astype(bf16)
        rest = to_table - high.astype(f32)
        mid = rest.astype(bf16)
        low = (rest - mid.astype(f32)).astype(bf16)
        to_pos = []
        for t in range(NEW):
            span = slice(t * HEADS, (t + 1) * HEADS)
            for part, piece in enumerate((high, mid, low)):
                pos_lhs[WIDTH + part * HEADS : WIDTH + (part + 1) * HEADS, :] = piece[span, :]
            halves = []
            for half in range(PIECE // TILE):
                cols = slice(half * TILE, (half + 1) * TILE)
                chosen = (
                    lax.broadcasted_iota(jnp.int32, (BUCKETS, TILE), 0)
                    == buckets_ref[t : t + 1, cols]
                ).astype(f32).astype(bf16)
                picked = jnp.dot(pos_lhs[...], chosen, preferred_element_type=f32)
                product = picked[0:WIDTH] * keys_t[:, cols]
                heads_sum = jnp.sum(product.reshape(HEADS, HEAD_DIM, TILE), axis=1)
                for sub in range(TILE // LANES):
                    at = (half * (TILE // LANES) + sub) * table_rows + t * HEADS
                    from_pos[at : at + HEADS, :] = heads_sum[:, sub * LANES : (sub + 1) * LANES]
                halves.append(
                    picked[WIDTH : WIDTH + HEADS]
                    + picked[WIDTH + HEADS : WIDTH + 2 * HEADS]
                    + picked[WIDTH + 2 * HEADS : WIDTH + 3 * HEADS]
                )
            to_pos.append(jnp.concatenate(halves, axis=1))
        from_parts = []
        for t in range(NEW):
            for j in range(2):
                from_parts.append(
                    jnp.concatenate(
                        [
                            from_pos[pl.ds(sub * table_rows + t * HEADS + j, CHUNKS, stride=2), :]
                            for sub in range(PIECE // LANES)
                        ],
                        axis=1,
                    )
                )
        total = content + jnp.concatenate(to_pos, axis=0) + jnp.concatenate(from_parts, axis=0)
        position = first + lax.broadcasted_iota(jnp.int32, (table_rows, PIECE), 1)
        allowed = (position < length) & ((position < SINKS) | (position >= start))
        scores = jnp.where(allowed, total * score_scale, masked_score)
        top = jnp.max(scores, axis=1, keepdims=True)
        weights = jnp.where(allowed, jnp.exp(scores - top), 0.0)
        sums = jnp.sum(weights, axis=1, keepdims=True)
        wide = jnp.dot(weights.astype(bf16), values_ref[...], preferred_element_type=f32)
        numer = jnp.sum(
            jnp.where(own_head, wide.reshape(NEW, HEADS, WIDTH), 0.0), axis=1
        )
        rows_to_tiles(numer, stage, NEW)
        for pair in range(2):
            msg_ref[pair, 0 : 2 * CHUNKS, :] = stage[
                pair * 2 * CHUNKS : (pair + 1) * 2 * CHUNKS, :
            ]
            columns = []
            for token in (2 * pair, 2 * pair + 1):
                for j in range(2):
                    at = token * HEADS + j * CHUNKS
                    columns.append(top[at : at + CHUNKS])
                    columns.append(sums[at : at + CHUNKS])
            msg_ref[pair, 2 * CHUNKS : MSG, :] = pack_ml(columns, lane)

    @pl.when(r == place_ref[0] // 2)
    def _():
        odd = lax.rem(place_ref[0], 2)
        q4 = proj[r, :, 0:WIDTH]
        k4 = proj[r, :, WIDTH : 2 * WIDTH]
        v4 = proj[r, :, 2 * WIDTH : 3 * WIDTH]
        wanted = new_ref[...]
        picked = (
            lax.broadcasted_iota(jnp.int32, (NEW * NEW, BUCKETS), 1) == wanted
        ).astype(f32).astype(bf16)
        pq = dot_nt(picked, pos_lhs[0:WIDTH, :])
        pk = jnp.dot(picked, pos_key[...], preferred_element_type=f32)
        q16 = jnp.broadcast_to(q4[:, None, :], (NEW, NEW, WIDTH)).reshape(NEW * NEW, WIDTH)
        k16 = jnp.broadcast_to(k4[None], (NEW, NEW, WIDTH)).reshape(NEW * NEW, WIDTH)
        rows_to_tiles(q16 * (k16 + pk) + k16 * pq, fresh_stage, NEW * NEW)
        rows_to_tiles(v4, stage, NEW)
        columns = []
        for i in range(2):
            token = 2 * odd + i
            spread = []
            for u in range(NEW):
                at = pl.multiple_of((token * NEW + u) * CHUNKS, CHUNKS)
                terms = fresh_stage[pl.ds(at, CHUNKS), :]
                even = jnp.sum(jnp.where(lane < HEAD_DIM, terms, 0.0), axis=1, keepdims=True)
                other = jnp.sum(jnp.where(lane >= HEAD_DIM, terms, 0.0), axis=1, keepdims=True)
                spread.append(
                    jnp.where(u <= token, spread_pair(even, other, lane) * score_scale, masked_score)
                )
            top = functools.reduce(jnp.maximum, spread)
            sums = jnp.zeros_like(top)
            numer = jnp.zeros_like(top)
            for u in range(NEW):
                weight = jnp.where(u <= token, jnp.exp(spread[u] - top), 0.0)
                sums = sums + weight
                numer = numer + weight.astype(bf16).astype(f32) * stage[
                    u * CHUNKS : (u + 1) * CHUNKS, :
                ]
            fresh_ref[i * CHUNKS : (i + 1) * CHUNKS, :] = numer
            for at in (0, HEAD_DIM):
                columns.append(top[:, at : at + 1])
                columns.append(sums[:, at : at + 1])
        fresh_ref[2 * CHUNKS : MSG, :] = pack_ml(columns, lane)


def attend_call(
    lengths, starts, place, hidden, rel, gains, biases, w_qkv, keys, values, buckets, new_buckets
):
    def whole(shape):
        return pl.BlockSpec(shape, lambda r, *_: (0,) * len(shape), pipeline_mode=pl.Buffered(1))

    return pl.pallas_call(
        attend_kernel,
        out_shape=(
            jax.ShapeDtypeStruct((SEQ_N, MSG, LANES), f32),
            jax.ShapeDtypeStruct((MSG, LANES), f32),
        ),
        grid_spec=pltpu.PrefetchScalarGridSpec(
            num_scalar_prefetch=3,
            grid=(GROUP,),
            in_specs=[
                whole((ROWS, WIDTH)),
                whole((BUCKETS, WIDTH)),
                whole((4, WIDTH)),
                whole((4, WIDTH)),
                whole((WIDTH, 3 * WIDTH)),
                pl.BlockSpec((None, PIECE, WIDTH), lambda r, *_: (r, 0, 0)),
                pl.BlockSpec((None, PIECE, WIDTH), lambda r, *_: (r, 0, 0)),
                pl.BlockSpec((None, NEW, PIECE), lambda r, *_: (r, 0, 0)),
                pl.BlockSpec((None, NEW * NEW, 1), lambda r, *_: (r, 0, 0)),
            ],
            out_specs=(
                pl.BlockSpec((2, MSG, LANES), lambda r, *_: (r, 0, 0)),
                pl.BlockSpec((MSG, LANES), lambda r, *_: (0, 0)),
            ),
            scratch_shapes=[
                pltpu.VMEM((GROUP, NEW, 3 * WIDTH), f32),
                pltpu.VMEM((WIDTH + 3 * HEADS, BUCKETS), bf16),
                pltpu.VMEM((BUCKETS, WIDTH), bf16),
                pltpu.VMEM((WIDTH, PIECE), f32),
                pltpu.VMEM((PIECE // LANES * NEW * HEADS, LANES), f32),
                pltpu.VMEM((NEW * CHUNKS, LANES), f32),
                pltpu.VMEM((NEW * NEW * CHUNKS, LANES), f32),
            ],
        ),
        compiler_params=pltpu.CompilerParams(vmem_limit_bytes=56 << 20),
        name="attend_piece",
    )(lengths, starts, place, hidden, rel, gains, biases, w_qkv, keys, values, buckets, new_buckets)


def finish_kernel(
    msg_ref, fresh_ref, hidden_ref, gain_ref, bias_ref, w_out_ref, w_in_ref, w_down_ref,
    out_ref, land, tiles, got, stage, rows_f,
    a_send, a_recv, b_send, b_recv, c_send, c_recv, d_send, d_recv,
):
    me = lax.axis_index("seq")
    barrier = pltpu.get_barrier_semaphore()
    for k in range(1, SEQ_N):
        pl.semaphore_signal(
            barrier, inc=1, device_id={"seq": lax.rem(me + k, SEQ_N)}, device_id_type=MESH
        )
    pl.semaphore_wait(barrier, SEQ_N - 1)
    lane = lax.broadcasted_iota(jnp.int32, (CHUNKS, LANES), 1)
    copies = seq_scatter(me, msg_ref, land, a_send, a_recv)
    land[0] = msg_ref[me]
    wait_all(copies)
    sources = [land.at[k] for k in range(SEQ_N)] + [fresh_ref]
    for i in range(2):
        tops, sums = [], []
        for source in sources:
            ml = source[2 * CHUNKS : MSG, :]
            at = i * HEAD_DIM
            tops.append(spread_pair(ml[:, at : at + 1], ml[:, at + 32 : at + 33], lane))
            sums.append(spread_pair(ml[:, at + 16 : at + 17], ml[:, at + 48 : at + 49], lane))
        top = functools.reduce(jnp.maximum, tops)
        numer = jnp.zeros_like(top)
        denom = jnp.zeros_like(top)
        for source, one, part in zip(sources, tops, sums):
            factor = jnp.exp(one - top)
            numer = numer + factor * source[i * CHUNKS : (i + 1) * CHUNKS, :]
            denom = denom + factor * part
        rows_f[i * CHUNKS : (i + 1) * CHUNKS, :] = numer / denom
    attended = tiles_to_rows(rows_f, 2).astype(bf16)
    rows_f[...] = hidden_ref[me].astype(f32)
    hidden_zero = tiles_to_rows(rows_f, 2)
    attn_out = jnp.dot(attended, w_out_ref[...], preferred_element_type=f32)
    hidden_one = (
        layer_norm(hidden_zero + attn_out, gain_ref[1:2, :], bias_ref[1:2, :])
        .astype(bf16)
        .astype(f32)
    )
    rows_to_tiles(hidden_one, rows_f, 2)
    tiles[0, me] = rows_f[...].astype(bf16)
    wait_all(seq_gather(me, tiles.at[0], b_send, b_recv))
    stage[...] = tiles[0].astype(f32).reshape(ROWS * CHUNKS, LANES)
    everyone = tiles_to_rows(stage, ROWS).astype(bf16)
    inner = dot_nt(everyone, w_in_ref[...])
    inner = (0.5 * inner * (1.0 + lax.erf(inner * math.sqrt(0.5)))).astype(bf16)
    rows_to_tiles(jnp.dot(inner, w_down_ref[...], preferred_element_type=f32), stage, ROWS)
    tiles[1] = stage[...].reshape(SEQ_N, 2 * CHUNKS, LANES).astype(bf16)
    copies = seq_scatter(me, tiles.at[1], got, c_send, c_recv)
    total = tiles[1, me].astype(f32)
    for k in range(1, SEQ_N):
        copies[k - 1].wait()
        total = total + got[k].astype(f32)
    rows_f[...] = total
    mlp_out = tiles_to_rows(rows_f, 2)
    layer_out = layer_norm(hidden_one + mlp_out, gain_ref[2:3, :], bias_ref[2:3, :])
    rows_to_tiles(layer_out, rows_f, 2)
    tiles[2, me] = rows_f[...].astype(bf16)
    wait_all(seq_gather(me, tiles.at[2], d_send, d_recv))
    stage[...] = tiles[2].astype(f32).reshape(ROWS * CHUNKS, LANES)
    out_ref[...] = tiles_to_rows(stage, ROWS).astype(bf16)


def finish_call(msg, fresh, hidden, gains, biases, w_out, w_in, w_down):
    slot = (SEQ_N, 2 * CHUNKS, LANES)
    return pl.pallas_call(
        finish_kernel,
        out_shape=jax.ShapeDtypeStruct((ROWS, WIDTH), bf16),
        in_specs=[pl.BlockSpec(memory_space=pltpu.VMEM)] * 8,
        out_specs=pl.BlockSpec(memory_space=pltpu.VMEM),
        scratch_shapes=[
            pltpu.VMEM((SEQ_N, MSG, LANES), f32),
            pltpu.VMEM((3,) + slot, bf16),
            pltpu.VMEM(slot, bf16),
            pltpu.VMEM((ROWS * CHUNKS, LANES), f32),
            pltpu.VMEM((2 * CHUNKS, LANES), f32),
        ]
        + [pltpu.SemaphoreType.DMA((SEQ_N,))] * 8,
        compiler_params=pltpu.CompilerParams(
            collective_id=1, has_side_effects=True, vmem_limit_bytes=32 << 20
        ),
        name="finish_layer",
    )(msg, fresh, hidden, gains, biases, w_out, w_in, w_down)


def shards(
    token_ids,
    embed_table,
    ln_gains,
    ln_biases,
    rel_table,
    w_qkv,
    w_out,
    cache_keys,
    cache_values,
    lengths,
    window_starts,
    cache_buckets,
    new_buckets,
    w_in,
    w_down,
):
    place = lax.axis_index("seq").astype(jnp.int32).reshape(1)
    hidden_zero = embed_call(token_ids.reshape(-1, 1), embed_table, ln_gains, ln_biases)
    messages, fresh = attend_call(
        lengths, window_starts, place, hidden_zero, rel_table, ln_gains, ln_biases, w_qkv,
        cache_keys, cache_values, cache_buckets, new_buckets.reshape(GROUP, NEW * NEW, 1),
    )
    hidden_tiles = hidden_zero.reshape(SEQ_N, 2 * CHUNKS, LANES)
    layer_out = finish_call(
        messages, fresh, hidden_tiles, ln_gains, ln_biases, w_out, w_in, w_down
    )
    return layer_out.reshape(GROUP, NEW, WIDTH)


def solution(mesh):
    in_specs = (
        P(),
        P(("req", "seq"), None),
        P(),
        P(),
        P(),
        P(),
        P(),
        P("req", "seq", None),
        P("req", "seq", None),
        P("req"),
        P("req"),
        P("req", None, "seq"),
        P("req", None, None),
        P("seq", None),
        P("seq", None),
    )
    out_specs = P("req", None, None)
    return jax.shard_map(shards, mesh=mesh, in_specs=in_specs, out_specs=out_specs, check_vma=False)
```

```python
import functools
import math

import jax
import jax.numpy as jnp
from jax import lax
from jax.experimental import pallas as pl
from jax.experimental.pallas import tpu as pltpu
from jax.sharding import PartitionSpec as P

HEADS = 16
HEAD_DIM = 64
SINKS = 4
NEW = 4
WIDTH = 1024
REQ_N = 8
SEQ_N = 16
GROUP = 8
ROWS = GROUP * NEW
PIECE = 512
BUCKETS = 512
TILE = 256
LANES = 128
CHUNKS = WIDTH // LANES
MSG = 24
HOOKS = (2, 3, 4)

norm_epsilon = 1e-06
masked_score = -1e30
score_scale = 1.0 / math.sqrt(3 * HEAD_DIM)
MESH = pl.DeviceIdType.MESH
f32 = jnp.float32
bf16 = jnp.bfloat16


def layer_norm(values, gain, shift):
    center = values - jnp.mean(values, axis=-1, keepdims=True)
    spread = jnp.mean(center * center, axis=-1, keepdims=True)
    return center * lax.rsqrt(spread + norm_epsilon) * gain + shift


def dot_nt(a, b):
    return lax.dot_general(a, b, (((1,), (1,)), ((), ())), preferred_element_type=f32)


def rows_to_tiles(rows, stage, count):
    for c in range(CHUNKS):
        stage[pl.ds(c, count, stride=CHUNKS), :] = rows[:, c * LANES : (c + 1) * LANES]


def tiles_to_rows(stage, count):
    return jnp.concatenate(
        [stage[pl.ds(c, count, stride=CHUNKS), :] for c in range(CHUNKS)], axis=1
    )


def seq_copy(src, dst, send_sem, recv_sem, peer):
    return pltpu.make_async_remote_copy(
        src_ref=src,
        dst_ref=dst,
        send_sem=send_sem,
        recv_sem=recv_sem,
        device_id={"seq": peer},
        device_id_type=MESH,
    )


def seq_scatter(me, send, recv, send_sems, recv_sems):
    copies = []
    for k in range(1, SEQ_N):
        peer = lax.rem(me + k, SEQ_N)
        copy = seq_copy(send.at[peer], recv.at[k], send_sems.at[k], recv_sems.at[k], peer)
        copies.append(copy)
    return copies


def seq_gather(me, buf, send_sems, recv_sems):
    copies = []
    for k in range(1, SEQ_N):
        peer = lax.rem(me + k, SEQ_N)
        copy = seq_copy(buf.at[me], buf.at[me], send_sems.at[k], recv_sems.at[k], peer)
        copies.append(copy)
    return copies


def start_all(copies):
    for copy in copies:
        copy.start()


def wait_all(copies):
    for copy in copies:
        copy.wait()


def spread_pair(column_even, column_odd, lane):
    return jnp.where(lane < HEAD_DIM, column_even, column_odd)


def pack_ml(values, lane):
    out = jnp.zeros((CHUNKS, LANES), f32)
    for g, value in enumerate(values):
        out = jnp.where((lane >> 4) == g, value, out)
    return out


def layer_kernel(
    ids_ref, table_hbm, gain_ref, bias_ref, rel_hbm, w_hbm, w_out_hbm, keys_hbm, values_hbm,
    lengths_ref, starts_ref, buckets_ref, new_ref, w_in_hbm, w_down_hbm,
    out_ref,
    table, rel, w_qkv, w_out, keys, values, w_in, w_down,
    send, land, stage, tiles, got, hid, rows_f, proj, pos_lhs, pos_key, keys_t, from_pos, queries,
    q_table, msgs, inbox, fresh, fresh_stage, picks,
    local_sems, key_sems, value_sems,
    req_send, req_recv, rs_send, rs_recv, ag_send, ag_recv,
    a_send, a_recv, b_send, b_recv, c_send, c_recv, d_send, d_recv,
):
    me = lax.axis_index("seq")
    req = lax.axis_index("req")
    table_rows = NEW * HEADS
    lane = lax.broadcasted_iota(jnp.int32, (CHUNKS, LANES), 1)

    def local(src, dst, index):
        return pltpu.make_async_copy(src, dst, local_sems.at[index])

    table_copy = local(table_hbm, table, 0)
    rel_copy = local(rel_hbm, rel, 1)
    w_copy = local(w_hbm, w_qkv, 2)
    out_copy = local(w_out_hbm, w_out, 3)
    in_copy = local(w_in_hbm, w_in, 4)
    down_copy = local(w_down_hbm, w_down, 5)

    def key_copy(r):
        return pltpu.make_async_copy(keys_hbm.at[r], keys.at[r], key_sems.at[r])

    def value_copy(r):
        return pltpu.make_async_copy(values_hbm.at[r], values.at[r], value_sems.at[r])

    table_copy.start()
    rel_copy.start()
    w_copy.start()
    barrier = pltpu.get_barrier_semaphore()
    for k in range(1, SEQ_N):
        pl.semaphore_signal(
            barrier, inc=1, device_id={"seq": lax.rem(me + k, SEQ_N)}, device_id_type=MESH
        )
    for k in range(1, REQ_N):
        pl.semaphore_signal(
            barrier, inc=1, device_id={"req": lax.rem(req + k, REQ_N)}, device_id_type=MESH
        )
    for r in range(GROUP):
        key_copy(r).start()

    vocab_rows = table.shape[0]
    ids = jnp.concatenate(
        [
            ids_ref[g * GROUP : (g + 1) * GROUP, t : t + 1]
            for g in range(REQ_N)
            for t in range(NEW)
        ],
        axis=0,
    ) - (req * SEQ_N + me) * vocab_rows
    one_hot = (
        lax.broadcasted_iota(jnp.int32, (REQ_N * ROWS, vocab_rows), 1) == ids
    ).astype(f32).astype(bf16)
    table_copy.wait()
    send[...] = (
        jnp.dot(one_hot, table[...], preferred_element_type=f32)
        .astype(bf16)
        .reshape(REQ_N, ROWS, WIDTH)
    )
    pl.semaphore_wait(barrier, SEQ_N - 1 + REQ_N - 1)

    def req_copies():
        copies = []
        for k in range(1, REQ_N):
            peer = lax.rem(req + k, REQ_N)
            copies.append(
                pltpu.make_async_remote_copy(
                    src_ref=send.at[peer],
                    dst_ref=land.at[k],
                    send_sem=req_send.at[k],
                    recv_sem=req_recv.at[k],
                    device_id={"req": peer},
                    device_id_type=MESH,
                )
            )
        return copies

    for copy in req_copies():
        copy.start()
    for r in range(GROUP):
        value_copy(r).start()
    out_copy.start()
    in_copy.start()
    down_copy.start()

    rel_copy.wait()
    relative = layer_norm(rel[...].astype(f32), gain_ref[3:4, :], bias_ref[3:4, :]).astype(bf16)
    flip = (
        lax.broadcasted_iota(jnp.int32, (BUCKETS, BUCKETS), 0)
        + lax.broadcasted_iota(jnp.int32, (BUCKETS, BUCKETS), 1)
        == BUCKETS - 1
    ).astype(f32).astype(bf16)
    flipped = jnp.dot(flip, relative, preferred_element_type=f32).astype(bf16)
    w_copy.wait()
    pos_lhs[...] = (
        jnp.dot(flipped, w_qkv[:, 0:WIDTH], preferred_element_type=f32).astype(bf16).T
    )
    pos_key[...] = jnp.dot(
        relative, w_qkv[:, WIDTH : 2 * WIDTH], preferred_element_type=f32
    ).astype(bf16)

    def own_head():
        row = lax.broadcasted_iota(jnp.int32, (NEW, HEADS, WIDTH), 1)
        col_head = lax.broadcasted_iota(jnp.int32, (NEW, HEADS, WIDTH), 2) >> 6
        return 2 * (row & (CHUNKS - 1)) + (row >> 3) == col_head

    def from_pos_step(r, carry):
        @pl.when(r == HOOKS[0])
        def _():
            copies = req_copies()
            total = send[req].astype(f32)
            for k in range(1, REQ_N):
                copies[k - 1].wait()
                total = total + land[k].astype(f32)
            for t in range(NEW):
                for c in range(CHUNKS):
                    stage[pl.ds(t * CHUNKS + c, GROUP, stride=NEW * CHUNKS), :] = total[
                        t * GROUP : (t + 1) * GROUP, c * LANES : (c + 1) * LANES
                    ]
            tiles[0] = stage[...].reshape(SEQ_N, 2 * CHUNKS, LANES).astype(bf16)
            start_all(seq_scatter(me, tiles.at[0], got.at[0], rs_send, rs_recv))

        @pl.when(r == HOOKS[1])
        def _():
            copies = seq_scatter(me, tiles.at[0], got.at[0], rs_send, rs_recv)
            own = tiles[0, me].astype(f32)
            for k in range(1, SEQ_N):
                copies[k - 1].wait()
                own = own + got[0, k].astype(f32)
            rows_f[...] = own
            hidden = layer_norm(tiles_to_rows(rows_f, 2), gain_ref[0:1, :], bias_ref[0:1, :])
            rows_to_tiles(hidden, rows_f, 2)
            hid[0, me] = rows_f[...].astype(bf16)
            start_all(seq_gather(me, hid.at[0], ag_send, ag_recv))

        @pl.when(r == HOOKS[2])
        def _():
            wait_all(seq_gather(me, hid.at[0], ag_send, ag_recv))
            stage[...] = hid[0].astype(f32).reshape(ROWS * CHUNKS, LANES)
            hidden = tiles_to_rows(stage, ROWS).astype(bf16)
            projected = (
                jnp.dot(hidden, w_qkv[...], preferred_element_type=f32).astype(bf16).astype(f32)
            )
            mine = own_head()
            for one in range(GROUP):
                block = projected[one * NEW : (one + 1) * NEW, :]
                proj[one] = block
                q_all = jnp.broadcast_to(block[:, None, 0:WIDTH], (NEW, HEADS, WIDTH))
                queries[one * table_rows : (one + 1) * table_rows, :] = (
                    jnp.where(mine, q_all, 0.0).reshape(table_rows, WIDTH).astype(bf16)
                )
            q_table[...] = dot_nt(queries[...], pos_key[...])

        key_copy(r).wait()
        keys_t[...] = keys[r].T.astype(f32)
        for t in range(NEW):
            for half in range(PIECE // TILE):
                cols = slice(half * TILE, (half + 1) * TILE)
                chosen = (
                    lax.broadcasted_iota(jnp.int32, (BUCKETS, TILE), 0)
                    == buckets_ref[r, t : t + 1, cols]
                ).astype(f32).astype(bf16)
                product = (
                    jnp.dot(pos_lhs[...], chosen, preferred_element_type=f32) * keys_t[:, cols]
                )
                heads_sum = jnp.sum(product.reshape(HEADS, HEAD_DIM, TILE), axis=1)
                for sub in range(TILE // LANES):
                    at = (half * (TILE // LANES) + sub) * table_rows + t * HEADS
                    from_pos[r, at : at + HEADS, :] = heads_sum[
                        :, sub * LANES : (sub + 1) * LANES
                    ]
        return carry

    lax.fori_loop(0, GROUP, from_pos_step, 0)

    first = me * PIECE

    def message_copy(r, pair):
        peer = 2 * r + pair
        return seq_copy(
            msgs.at[peer], inbox.at[me], a_send.at[peer], a_recv.at[me], peer
        )

    def attend_step(r, carry):
        value_copy(r).wait()
        span = pl.ds(pl.multiple_of(r * table_rows, table_rows), table_rows)
        content = dot_nt(queries[span, :], keys[r])
        parts = []
        for t in range(NEW):
            tables = [
                q_table[
                    pl.ds(pl.multiple_of(r * table_rows + t * HEADS, HEADS), HEADS),
                    kb * LANES : (kb + 1) * LANES,
                ]
                for kb in range(BUCKETS // LANES)
            ]
            columns = []
            for sub in range(PIECE // LANES):
                bucket = jnp.broadcast_to(
                    buckets_ref[r, t : t + 1, sub * LANES : (sub + 1) * LANES], (HEADS, LANES)
                )
                low = bucket & (LANES - 1)
                high = bucket >> 7
                picked = jnp.take_along_axis(tables[0], low, axis=1)
                for kb in range(1, BUCKETS // LANES):
                    picked = jnp.where(
                        high == kb, jnp.take_along_axis(tables[kb], low, axis=1), picked
                    )
                back = jnp.concatenate(
                    [
                        from_pos[
                            r, pl.ds(sub * table_rows + t * HEADS + j, CHUNKS, stride=2), :
                        ]
                        for j in range(2)
                    ],
                    axis=0,
                )
                columns.append(picked + back)
            parts.append(jnp.concatenate(columns, axis=1))
        total = content + jnp.concatenate(parts, axis=0)
        position = first + lax.broadcasted_iota(jnp.int32, (table_rows, PIECE), 1)
        allowed = (position < lengths_ref[r]) & (
            (position < SINKS) | (position >= starts_ref[r])
        )
        scores = jnp.where(allowed, total * score_scale, masked_score)
        top = jnp.max(scores, axis=1, keepdims=True)
        weights = jnp.where(allowed, jnp.exp(scores - top), 0.0)
        sums = jnp.sum(weights, axis=1, keepdims=True)
        wide = jnp.dot(weights.astype(bf16), values[r], preferred_element_type=f32)
        numer = jnp.sum(jnp.where(own_head(), wide.reshape(NEW, HEADS, WIDTH), 0.0), axis=1)
        rows_to_tiles(numer, stage, NEW)
        for pair in range(2):
            peer = 2 * r + pair
            msgs[peer, 0 : 2 * CHUNKS, :] = stage[
                pair * 2 * CHUNKS : (pair + 1) * 2 * CHUNKS, :
            ]
            columns = []
            for token in (2 * pair, 2 * pair + 1):
                for j in range(2):
                    at = token * HEADS + j * CHUNKS
                    columns.append(top[at : at + CHUNKS])
                    columns.append(sums[at : at + CHUNKS])
            msgs[peer, 2 * CHUNKS : MSG, :] = pack_ml(columns, lane)

            @pl.when(peer != me)
            def _():
                message_copy(r, pair).start()

        return carry

    lax.fori_loop(0, GROUP, attend_step, 0)

    odd = lax.rem(me, 2)
    mine = proj[me // 2]
    wanted = new_ref[me // 2]
    for t in range(NEW):
        picks[t * NEW : (t + 1) * NEW, :] = wanted[:, t : t + 1]
    picked = (
        lax.broadcasted_iota(jnp.int32, (NEW * NEW, BUCKETS), 1) == picks[...]
    ).astype(f32).astype(bf16)
    pq = dot_nt(picked, pos_lhs[...])
    pk = jnp.dot(picked, pos_key[...], preferred_element_type=f32)
    q4, k4, v4 = (mine[:, i * WIDTH : (i + 1) * WIDTH] for i in range(3))
    q16 = jnp.broadcast_to(q4[None], (NEW, NEW, WIDTH)).reshape(NEW * NEW, WIDTH)
    k16 = jnp.broadcast_to(k4[:, None, :], (NEW, NEW, WIDTH)).reshape(NEW * NEW, WIDTH)
    rows_to_tiles(q16 * (k16 + pk) + k16 * pq, fresh_stage, NEW * NEW)
    rows_to_tiles(v4, stage, NEW)
    columns = []
    for i in range(2):
        token = 2 * odd + i
        spread = []
        for u in range(NEW):
            at = pl.multiple_of((u * NEW + token) * CHUNKS, CHUNKS)
            terms = fresh_stage[pl.ds(at, CHUNKS), :]
            even = jnp.sum(jnp.where(lane < HEAD_DIM, terms, 0.0), axis=1, keepdims=True)
            other = jnp.sum(jnp.where(lane >= HEAD_DIM, terms, 0.0), axis=1, keepdims=True)
            spread.append(
                jnp.where(u <= token, spread_pair(even, other, lane) * score_scale, masked_score)
            )
        top = functools.reduce(jnp.maximum, spread)
        sums = jnp.zeros_like(top)
        numer = jnp.zeros_like(top)
        for u in range(NEW):
            weight = jnp.where(u <= token, jnp.exp(spread[u] - top), 0.0)
            sums = sums + weight
            numer = numer + weight.astype(bf16).astype(f32) * stage[
                u * CHUNKS : (u + 1) * CHUNKS, :
            ]
        fresh[i * CHUNKS : (i + 1) * CHUNKS, :] = numer
        for at in (0, HEAD_DIM):
            columns.append(top[:, at : at + 1])
            columns.append(sums[:, at : at + 1])
    fresh[2 * CHUNKS : MSG, :] = pack_ml(columns, lane)

    inbox[me] = msgs[me]
    for k in range(1, SEQ_N):
        peer = lax.rem(me + k, SEQ_N)
        seq_copy(
            msgs.at[peer], inbox.at[peer], a_send.at[peer], a_recv.at[peer], peer
        ).wait()
    sources = [inbox.at[k] for k in range(SEQ_N)] + [fresh]
    for i in range(2):
        tops, sums = [], []
        for source in sources:
            ml = source[2 * CHUNKS : MSG, :]
            at = i * HEAD_DIM
            tops.append(spread_pair(ml[:, at : at + 1], ml[:, at + 32 : at + 33], lane))
            sums.append(spread_pair(ml[:, at + 16 : at + 17], ml[:, at + 48 : at + 49], lane))
        top = functools.reduce(jnp.maximum, tops)
        numer = jnp.zeros_like(top)
        denom = jnp.zeros_like(top)
        for source, one, part in zip(sources, tops, sums):
            factor = jnp.exp(one - top)
            numer = numer + factor * source[i * CHUNKS : (i + 1) * CHUNKS, :]
            denom = denom + factor * part
        rows_f[i * CHUNKS : (i + 1) * CHUNKS, :] = numer / denom
    attended = tiles_to_rows(rows_f, 2).astype(bf16)
    rows_f[...] = hid[0, me].astype(f32)
    hidden_zero = tiles_to_rows(rows_f, 2)
    out_copy.wait()
    attn_out = jnp.dot(attended, w_out[...], preferred_element_type=f32)
    hidden_one = (
        layer_norm(hidden_zero + attn_out, gain_ref[1:2, :], bias_ref[1:2, :])
        .astype(bf16)
        .astype(f32)
    )
    rows_to_tiles(hidden_one, rows_f, 2)
    hid[1, me] = rows_f[...].astype(bf16)
    copies = seq_gather(me, hid.at[1], b_send, b_recv)
    start_all(copies)
    in_copy.wait()
    down_copy.wait()
    wait_all(copies)
    stage[...] = hid[1].astype(f32).reshape(ROWS * CHUNKS, LANES)
    everyone = tiles_to_rows(stage, ROWS).astype(bf16)
    inner = dot_nt(everyone, w_in[...])
    inner = (0.5 * inner * (1.0 + lax.erf(inner * math.sqrt(0.5)))).astype(bf16)
    rows_to_tiles(jnp.dot(inner, w_down[...], preferred_element_type=f32), stage, ROWS)
    tiles[1] = stage[...].reshape(SEQ_N, 2 * CHUNKS, LANES).astype(bf16)
    copies = seq_scatter(me, tiles.at[1], got.at[1], c_send, c_recv)
    start_all(copies)
    total = tiles[1, me].astype(f32)
    for k in range(1, SEQ_N):
        copies[k - 1].wait()
        total = total + got[1, k].astype(f32)
    rows_f[...] = total
    mlp_out = tiles_to_rows(rows_f, 2)
    layer_out = layer_norm(hidden_one + mlp_out, gain_ref[2:3, :], bias_ref[2:3, :])
    rows_to_tiles(layer_out, rows_f, 2)
    hid[2, me] = rows_f[...].astype(bf16)
    copies = seq_gather(me, hid.at[2], d_send, d_recv)
    start_all(copies)
    wait_all(copies)
    stage[...] = hid[2].astype(f32).reshape(ROWS * CHUNKS, LANES)
    everyone = tiles_to_rows(stage, ROWS)
    for r in range(GROUP):
        out_ref[r] = everyone[r * NEW : (r + 1) * NEW, :].astype(bf16)


def shards(
    token_ids,
    embed_table,
    ln_gains,
    ln_biases,
    rel_table,
    w_qkv,
    w_out,
    cache_keys,
    cache_values,
    lengths,
    window_starts,
    cache_buckets,
    new_buckets,
    w_in,
    w_down,
):
    slot = (SEQ_N, 2 * CHUNKS, LANES)
    in_vmem = pl.BlockSpec(memory_space=pltpu.VMEM)
    in_smem = pl.BlockSpec(memory_space=pltpu.SMEM)
    in_place = pl.BlockSpec(memory_space=pl.ANY)
    return pl.pallas_call(
        layer_kernel,
        out_shape=jax.ShapeDtypeStruct((GROUP, NEW, WIDTH), bf16),
        in_specs=[
            in_vmem, in_place, in_vmem, in_vmem, in_place, in_place, in_place, in_place, in_place,
            in_smem, in_smem, in_vmem, in_vmem, in_place, in_place,
        ],
        out_specs=in_vmem,
        scratch_shapes=[
            pltpu.VMEM(embed_table.shape, bf16),
            pltpu.VMEM(rel_table.shape, bf16),
            pltpu.VMEM(w_qkv.shape, bf16),
            pltpu.VMEM(w_out.shape, bf16),
            pltpu.VMEM(cache_keys.shape, bf16),
            pltpu.VMEM(cache_values.shape, bf16),
            pltpu.VMEM(w_in.shape, bf16),
            pltpu.VMEM(w_down.shape, bf16),
            pltpu.VMEM((REQ_N, ROWS, WIDTH), bf16),
            pltpu.VMEM((REQ_N, ROWS, WIDTH), bf16),
            pltpu.VMEM((ROWS * CHUNKS, LANES), f32),
            pltpu.VMEM((2,) + slot, bf16),
            pltpu.VMEM((2,) + slot, bf16),
            pltpu.VMEM((3,) + slot, bf16),
            pltpu.VMEM((2 * CHUNKS, LANES), f32),
            pltpu.VMEM((GROUP, NEW, 3 * WIDTH), f32),
            pltpu.VMEM((WIDTH, BUCKETS), bf16),
            pltpu.VMEM((BUCKETS, WIDTH), bf16),
            pltpu.VMEM((WIDTH, PIECE), f32),
            pltpu.VMEM((GROUP, PIECE // LANES * NEW * HEADS, LANES), f32),
            pltpu.VMEM((GROUP * NEW * HEADS, WIDTH), bf16),
            pltpu.VMEM((GROUP * NEW * HEADS, BUCKETS), f32),
            pltpu.VMEM((SEQ_N, MSG, LANES), f32),
            pltpu.VMEM((SEQ_N, MSG, LANES), f32),
            pltpu.VMEM((MSG, LANES), f32),
            pltpu.VMEM((NEW * NEW * CHUNKS, LANES), f32),
            pltpu.VMEM((NEW * NEW, 1), jnp.int32),
            pltpu.SemaphoreType.DMA((6,)),
            pltpu.SemaphoreType.DMA((GROUP,)),
            pltpu.SemaphoreType.DMA((GROUP,)),
        ]
        + [pltpu.SemaphoreType.DMA((REQ_N,))] * 2
        + [pltpu.SemaphoreType.DMA((SEQ_N,))] * 12,
        compiler_params=pltpu.CompilerParams(
            collective_id=0, has_side_effects=True, vmem_limit_bytes=60 << 20
        ),
        name="decode_layer",
    )(
        token_ids, embed_table, ln_gains, ln_biases, rel_table, w_qkv, w_out, cache_keys,
        cache_values, lengths, window_starts, cache_buckets, new_buckets, w_in, w_down,
    )


def solution(mesh):
    in_specs = (
        P(),
        P(("req", "seq"), None),
        P(),
        P(),
        P(),
        P(),
        P(),
        P("req", "seq", None),
        P("req", "seq", None),
        P("req"),
        P("req"),
        P("req", None, "seq"),
        P("req", None, None),
        P("seq", None),
        P("seq", None),
    )
    out_specs = P("req", None, None)
    return jax.shard_map(shards, mesh=mesh, in_specs=in_specs, out_specs=out_specs, check_vma=False)
```

```python
import functools
import math

import jax
import jax.numpy as jnp
from jax import lax
from jax.experimental import pallas as pl
from jax.experimental.pallas import tpu as pltpu
from jax.sharding import PartitionSpec as P

HEADS = 16
HEAD_DIM = 64
SINKS = 4
NEW = 4
WIDTH = 1024
REQ_N = 8
SEQ_N = 16
GROUP = 8
ROWS = GROUP * NEW
PIECE = 512
BUCKETS = 512
TILE = 256
LANES = 128
CHUNKS = WIDTH // LANES
SIDE = 4
HOOKS = (3, 5, 7)
FORWARD = 4

norm_epsilon = 1e-06
masked_score = -1e30
score_scale = 1.0 / math.sqrt(3 * HEAD_DIM)
MESH = pl.DeviceIdType.MESH
f32 = jnp.float32
bf16 = jnp.bfloat16


def layer_norm(values, gain, shift):
    center = values - jnp.mean(values, axis=-1, keepdims=True)
    spread = jnp.mean(center * center, axis=-1, keepdims=True)
    return center * lax.rsqrt(spread + norm_epsilon) * gain + shift


def dot_nt(a, b):
    return lax.dot_general(a, b, (((1,), (1,)), ((), ())), preferred_element_type=f32)


def rows_to_tiles(rows, stage, count):
    for c in range(CHUNKS):
        stage[pl.ds(c, count, stride=CHUNKS), :] = rows[:, c * LANES : (c + 1) * LANES]


def tiles_to_rows(stage, count):
    return jnp.concatenate(
        [stage[pl.ds(c, count, stride=CHUNKS), :] for c in range(CHUNKS)], axis=1
    )


def seq_copy(src, dst, send_sem, recv_sem, peer):
    return pltpu.make_async_remote_copy(
        src_ref=src,
        dst_ref=dst,
        send_sem=send_sem,
        recv_sem=recv_sem,
        device_id={"seq": peer},
        device_id_type=MESH,
    )


def seq_scatter(me, send, recv, send_sems, recv_sems):
    copies = []
    for k in range(1, SEQ_N):
        peer = lax.rem(me + k, SEQ_N)
        copy = seq_copy(send.at[peer], recv.at[k], send_sems.at[k], recv_sems.at[k], peer)
        copies.append(copy)
    return copies


def seq_gather(me, buf, send_sems, recv_sems):
    copies = []
    for k in range(1, SEQ_N):
        peer = lax.rem(me + k, SEQ_N)
        copy = seq_copy(buf.at[me], buf.at[me], send_sems.at[k], recv_sems.at[k], peer)
        copies.append(copy)
    return copies


def start_all(copies):
    for copy in copies:
        copy.start()


def wait_all(copies):
    for copy in copies:
        copy.wait()


def spread_pair(column_even, column_odd, lane):
    return jnp.where(lane < HEAD_DIM, column_even, column_odd)


def pack_ml(values, lane):
    out = jnp.zeros((CHUNKS, LANES), f32)
    for g, value in enumerate(values):
        out = jnp.where((lane >> 3) == g, value, out)
    return out


def layer_kernel(
    ids_ref, table_hbm, gain_ref, bias_ref, rel_hbm, w_hbm, w_out_hbm, keys_hbm, values_hbm,
    lengths_ref, starts_ref, buckets_ref, new_ref, w_in_hbm, w_down_hbm,
    out_ref,
    table, rel, w_qkv, w_out, keys, values, w_ff, ids_pad,
    send, land, stage, tiles, got, hid, h_zero, rows_f, att, proj, pos_lhs, pos_key, keys_t,
    from_pos, queries, q_table, msg_numer, msg_ml, in_numer, in_ml, fresh_numer, fresh_ml,
    fresh_stage, v_stage, picks, partial, final,
    local_sems, key_sems, value_sems,
    req_send, req_recv, rs_send, rs_recv, ag_send, ag_recv,
    n_send, n_recv, m_send, m_recv, w_send, w_recv, f_send, f_recv, y_send, y_recv, x_send, x_recv,
):
    me = lax.axis_index("seq")
    req = lax.axis_index("req")
    at_x, at_y = me // SIDE, lax.rem(me, SIDE)
    core = lax.rem(req, 2)
    table_rows = NEW * HEADS
    lane = lax.broadcasted_iota(jnp.int32, (CHUNKS, LANES), 1)

    def local(src, dst, index):
        return pltpu.make_async_copy(src, dst, local_sems.at[index])

    table_copy = local(table_hbm, table, 0)
    rel_copy = local(rel_hbm, rel, 1)
    w_copies = [
        local(
            w_hbm.at[:, i * WIDTH : (i + 1) * WIDTH], w_qkv.at[:, i * WIDTH : (i + 1) * WIDTH], 2 + i
        )
        for i in range(3)
    ]
    out_copy = local(w_out_hbm, w_out, 5)
    in_copy = local(w_in_hbm, w_ff.at[0, at_x], 6)
    down_copy = local(w_down_hbm, w_ff.at[1, at_x], 7)

    def key_copy(r):
        return pltpu.make_async_copy(keys_hbm.at[r], keys.at[r], key_sems.at[r])

    def value_copy(r):
        return pltpu.make_async_copy(values_hbm.at[r], values.at[r], value_sems.at[r])

    table_copy.start()
    rel_copy.start()
    w_copies[0].start()
    w_copies[1].start()
    barrier = pltpu.get_barrier_semaphore()
    for k in range(1, SEQ_N):
        pl.semaphore_signal(
            barrier, inc=1, device_id={"seq": lax.rem(me + k, SEQ_N)}, device_id_type=MESH
        )
    for k in range(1, REQ_N):
        pl.semaphore_signal(
            barrier, inc=1, device_id={"req": lax.rem(req + k, REQ_N)}, device_id_type=MESH
        )
    key_copy(0).start()
    in_copy.start()
    down_copy.start()

    vocab_rows = table.shape[0]
    ids_pad[...] = jnp.zeros((8, LANES), jnp.int32)
    ids_pad[0:NEW, 0 : REQ_N * GROUP] = ids_ref[...]
    ids_t = ids_pad[...].T
    ids = jnp.concatenate(
        [
            ids_t[g * GROUP : (g + 1) * GROUP, t : t + 1]
            for g in range(REQ_N)
            for t in range(NEW)
        ],
        axis=0,
    ) - (req * SEQ_N + me) * vocab_rows
    one_hot = (
        lax.broadcasted_iota(jnp.int32, (REQ_N * ROWS, vocab_rows), 1) == ids
    ).astype(f32).astype(bf16)
    table_copy.wait()
    send[...] = (
        jnp.dot(one_hot, table[...], preferred_element_type=f32)
        .astype(bf16)
        .reshape(REQ_N, ROWS, WIDTH)
    )
    pl.semaphore_wait(barrier, SEQ_N - 1 + REQ_N - 1)

    def req_copies():
        copies = []
        for k in range(1, REQ_N):
            peer = lax.rem(req + k, REQ_N)
            copies.append(
                pltpu.make_async_remote_copy(
                    src_ref=send.at[peer],
                    dst_ref=land.at[k],
                    send_sem=req_send.at[k],
                    recv_sem=req_recv.at[k],
                    device_id={"req": peer},
                    device_id_type=MESH,
                )
            )
        return copies

    for copy in req_copies():
        copy.start()

    rel_copy.wait()
    relative = layer_norm(rel[...].astype(f32), gain_ref[3:4, :], bias_ref[3:4, :]).astype(bf16)
    flip = (
        lax.broadcasted_iota(jnp.int32, (BUCKETS, BUCKETS), 0)
        + lax.broadcasted_iota(jnp.int32, (BUCKETS, BUCKETS), 1)
        == BUCKETS - 1
    ).astype(f32).astype(bf16)
    flipped = jnp.dot(flip, relative, preferred_element_type=f32).astype(bf16)
    w_copies[0].wait()
    pos_lhs[...] = (
        jnp.dot(flipped, w_qkv[:, 0:WIDTH], preferred_element_type=f32).astype(bf16).T
    )
    w_copies[1].wait()
    key_copy(1).start()
    w_copies[2].start()
    pos_key[...] = jnp.dot(
        relative, w_qkv[:, WIDTH : 2 * WIDTH], preferred_element_type=f32
    ).astype(bf16)

    def own_head():
        row = lax.broadcasted_iota(jnp.int32, (NEW, HEADS, WIDTH), 1)
        col_head = lax.broadcasted_iota(jnp.int32, (NEW, HEADS, WIDTH), 2) >> 6
        return 2 * (row & (CHUNKS - 1)) + (row >> 3) == col_head

    def near_copy(src, dst, send_sem, recv_sem, axis, peer):
        return pltpu.make_async_remote_copy(
            src_ref=src,
            dst_ref=dst,
            send_sem=send_sem,
            recv_sem=recv_sem,
            device_id={axis: peer},
            device_id_type=MESH,
        )

    def x_peer(k):
        return lax.rem(at_x + k, SIDE) * SIDE + at_y

    def y_peer(k):
        return at_x * SIDE + lax.rem(at_y + k, SIDE)

    def shard_copies():
        held = w_ff.at[core, at_x]
        return [
            near_copy(held, held, w_send.at[k], w_recv.at[k], "seq", x_peer(k))
            for k in range(1, SIDE)
        ]

    def forward_copies():
        copies = []
        for k in range(1, SIDE):
            held = w_ff.at[core, lax.rem(at_x + k, SIDE)]
            copies.append(
                near_copy(held, held, f_send.at[k], f_recv.at[k], "req", req + 1 - 2 * core)
            )
        return copies

    def from_pos_step(r, carry):
        value_copy(r).start()

        @pl.when(r < GROUP - 2)
        def _():
            key_copy(r + 2).start()

        @pl.when(r == 0)
        def _():
            in_copy.wait()
            down_copy.wait()
            out_copy.start()
            start_all(shard_copies())

        @pl.when(r == HOOKS[0])
        def _():
            copies = req_copies()
            total = send[req].astype(f32)
            for k in range(1, REQ_N):
                copies[k - 1].wait()
                total = total + land[k].astype(f32)
            for t in range(NEW):
                for c in range(CHUNKS):
                    stage[pl.ds(t * CHUNKS + c, GROUP, stride=NEW * CHUNKS), :] = total[
                        t * GROUP : (t + 1) * GROUP, c * LANES : (c + 1) * LANES
                    ]
            tiles[0] = stage[...].reshape(SEQ_N, 2 * CHUNKS, LANES).astype(bf16)
            start_all(seq_scatter(me, tiles.at[0], got.at[0], rs_send, rs_recv))

        @pl.when(r == HOOKS[1])
        def _():
            copies = seq_scatter(me, tiles.at[0], got.at[0], rs_send, rs_recv)
            own = tiles[0, me].astype(f32)
            for k in range(1, SEQ_N):
                copies[k - 1].wait()
                own = own + got[0, k].astype(f32)
            rows_f[...] = own
            hidden = layer_norm(tiles_to_rows(rows_f, 2), gain_ref[0:1, :], bias_ref[0:1, :])
            rows_to_tiles(hidden, rows_f, 2)
            hid[0, me] = rows_f[...].astype(bf16)
            start_all(seq_gather(me, hid.at[0], ag_send, ag_recv))

        @pl.when(r == HOOKS[2])
        def _():
            wait_all(seq_gather(me, hid.at[0], ag_send, ag_recv))
            stage[...] = hid[0].astype(f32).reshape(ROWS * CHUNKS, LANES)
            hidden = tiles_to_rows(stage, ROWS)
            for one in range(SIDE):
                h_zero[one] = hidden[one * 2 * NEW : (one + 1) * 2 * NEW, :]
            hidden = hidden.astype(bf16)
            w_copies[2].wait()
            projected = (
                jnp.dot(hidden, w_qkv[...], preferred_element_type=f32).astype(bf16).astype(f32)
            )
            mine = own_head()
            for one in range(GROUP):
                block = projected[one * NEW : (one + 1) * NEW, :]
                proj[one] = block
                q_all = jnp.broadcast_to(block[:, None, 0:WIDTH], (NEW, HEADS, WIDTH))
                queries[one * table_rows : (one + 1) * table_rows, :] = (
                    jnp.where(mine, q_all, 0.0).reshape(table_rows, WIDTH).astype(bf16)
                )
            q_table[...] = dot_nt(queries[...], pos_key[...])

        key_copy(r).wait()
        keys_t[...] = keys[r].T.astype(f32)
        for t in range(NEW):
            for half in range(PIECE // TILE):
                cols = slice(half * TILE, (half + 1) * TILE)
                chosen = (
                    lax.broadcasted_iota(jnp.int32, (BUCKETS, TILE), 0)
                    == buckets_ref[r, t : t + 1, cols]
                ).astype(f32).astype(bf16)
                product = (
                    jnp.dot(pos_lhs[...], chosen, preferred_element_type=f32) * keys_t[:, cols]
                )
                heads_sum = jnp.sum(product.reshape(HEADS, HEAD_DIM, TILE), axis=1)
                for sub in range(TILE // LANES):
                    at = (half * (TILE // LANES) + sub) * table_rows + t * HEADS
                    from_pos[r, at : at + HEADS, :] = heads_sum[
                        :, sub * LANES : (sub + 1) * LANES
                    ]
        return carry

    lax.fori_loop(0, GROUP, from_pos_step, 0)

    first = me * PIECE

    def message_copies(r, k):
        peer = (r // 2) * SIDE + k
        slot = lax.rem(peer - me + SEQ_N, SEQ_N) - 1
        part = lax.rem(r, 2)
        return peer, [
            near_copy(msg_numer.at[r], in_numer.at[slot, part], n_send, n_recv, "seq", peer),
            near_copy(msg_ml.at[r], in_ml.at[slot, part], m_send, m_recv, "seq", peer),
        ]

    def attend_step(r, carry):
        @pl.when(r == FORWARD)
        def _():
            wait_all(shard_copies())
            start_all(forward_copies())

        value_copy(r).wait()
        span = pl.ds(pl.multiple_of(r * table_rows, table_rows), table_rows)
        content = dot_nt(queries[span, :], keys[r])
        parts = []
        for t in range(NEW):
            tables = [
                q_table[
                    pl.ds(pl.multiple_of(r * table_rows + t * HEADS, HEADS), HEADS),
                    kb * LANES : (kb + 1) * LANES,
                ]
                for kb in range(BUCKETS // LANES)
            ]
            columns = []
            for sub in range(PIECE // LANES):
                bucket = jnp.broadcast_to(
                    buckets_ref[r, t : t + 1, sub * LANES : (sub + 1) * LANES], (HEADS, LANES)
                )
                low = bucket & (LANES - 1)
                high = bucket >> 7
                picked = jnp.take_along_axis(tables[0], low, axis=1)
                for kb in range(1, BUCKETS // LANES):
                    picked = jnp.where(
                        high == kb, jnp.take_along_axis(tables[kb], low, axis=1), picked
                    )
                back = jnp.concatenate(
                    [
                        from_pos[
                            r, pl.ds(sub * table_rows + t * HEADS + j, CHUNKS, stride=2), :
                        ]
                        for j in range(2)
                    ],
                    axis=0,
                )
                columns.append(picked + back)
            parts.append(jnp.concatenate(columns, axis=1))
        total = content + jnp.concatenate(parts, axis=0)
        position = first + lax.broadcasted_iota(jnp.int32, (table_rows, PIECE), 1)
        allowed = (position < lengths_ref[r]) & (
            (position < SINKS) | (position >= starts_ref[r])
        )
        scores = jnp.where(allowed, total * score_scale, masked_score)
        top = jnp.max(scores, axis=1, keepdims=True)
        weights = jnp.where(allowed, jnp.exp(scores - top), 0.0)
        sums = jnp.sum(weights, axis=1, keepdims=True)
        wide = jnp.dot(weights.astype(bf16), values[r], preferred_element_type=f32)
        numer = jnp.sum(jnp.where(own_head(), wide.reshape(NEW, HEADS, WIDTH), 0.0), axis=1)
        rows_to_tiles(numer, v_stage, NEW)
        msg_numer[r] = v_stage[0 : NEW * CHUNKS, :].astype(bf16)
        columns = []
        for token in range(NEW):
            for j in range(2):
                at = token * HEADS + j * CHUNKS
                columns.append(top[at : at + CHUNKS])
                columns.append(sums[at : at + CHUNKS])
        msg_ml[r] = pack_ml(columns, lane)
        for k in range(SIDE):
            peer, copies = message_copies(r, k)

            @pl.when(peer != me)
            def _():
                start_all(copies)

        return carry

    lax.fori_loop(0, GROUP, attend_step, 0)

    new_lane = lax.broadcasted_iota(jnp.int32, (NEW, NEW, GROUP), 2)
    new_all = new_ref[...].astype(f32)
    for i in range(2):
        wanted = jnp.sum(
            jnp.where(new_lane == 2 * at_x + i, new_all, 0.0), axis=2, keepdims=True
        )
        for t in range(NEW):
            at = (i * NEW + t) * NEW
            picks[at : at + NEW, :] = wanted[t]
    picked = (
        lax.broadcasted_iota(jnp.int32, (2 * NEW * NEW, BUCKETS), 1).astype(f32) == picks[...]
    ).astype(f32).astype(bf16)
    pq = dot_nt(picked, pos_lhs[...])
    pk = jnp.dot(picked, pos_key[...], preferred_element_type=f32)
    for i in range(2):
        mine = proj[2 * at_x + i]
        q4, k4, v4 = (mine[:, w * WIDTH : (w + 1) * WIDTH] for w in range(3))
        pairs = NEW * NEW
        q16 = jnp.broadcast_to(q4[:, None, :], (NEW, NEW, WIDTH)).reshape(pairs, WIDTH)
        k16 = jnp.broadcast_to(k4[None], (NEW, NEW, WIDTH)).reshape(pairs, WIDTH)
        span = slice(i * pairs, (i + 1) * pairs)
        rows_to_tiles(q16 * (k16 + pk[span]) + k16 * pq[span], fresh_stage, pairs)
        rows_to_tiles(v4, v_stage, NEW)
        columns = []
        for t in range(NEW):
            spread = []
            for u in range(t + 1):
                at = (t * NEW + u) * CHUNKS
                terms = fresh_stage[at : at + CHUNKS, :]
                even = jnp.sum(jnp.where(lane < HEAD_DIM, terms, 0.0), axis=1, keepdims=True)
                other = jnp.sum(jnp.where(lane >= HEAD_DIM, terms, 0.0), axis=1, keepdims=True)
                spread.append(spread_pair(even, other, lane) * score_scale)
            top = functools.reduce(jnp.maximum, spread)
            sums = jnp.zeros_like(top)
            numer = jnp.zeros_like(top)
            for u in range(t + 1):
                weight = jnp.exp(spread[u] - top)
                sums = sums + weight
                numer = numer + weight.astype(bf16).astype(f32) * v_stage[
                    u * CHUNKS : (u + 1) * CHUNKS, :
                ]
            fresh_numer[i, t * CHUNKS : (t + 1) * CHUNKS, :] = numer
            for at in (0, HEAD_DIM):
                columns.append(top[:, at : at + 1])
                columns.append(sums[:, at : at + 1])
        fresh_ml[i] = pack_ml(columns, lane)

    near_copy(in_numer, in_numer, n_send, n_recv, "seq", x_peer(1)).wait()
    near_copy(in_ml, in_ml, m_send, m_recv, "seq", x_peer(1)).wait()
    for i in range(2):
        mls = [in_ml[k, i] for k in range(SEQ_N - 1)] + [msg_ml[2 * at_x + i], fresh_ml[i]]
        top = functools.reduce(jnp.maximum, mls)
        factors = [jnp.exp(ml - top) for ml in mls]
        denom = functools.reduce(
            jnp.add, [f * pltpu.roll(ml, LANES - 8, axis=1) for f, ml in zip(factors, mls)]
        )
        numers = [jnp.zeros((CHUNKS, LANES), f32) for _ in range(NEW)]
        for k, factor in enumerate(factors):
            if k < SEQ_N - 1:
                block = in_numer[k, i].astype(f32)
            elif k == SEQ_N - 1:
                block = msg_numer[2 * at_x + i].astype(f32)
            else:
                block = fresh_numer[i]
            for t in range(NEW):
                at = t * 32
                numers[t] = numers[t] + block[t * CHUNKS : (t + 1) * CHUNKS] * spread_pair(
                    factor[:, at : at + 1], factor[:, at + 16 : at + 17], lane
                )
        for t in range(NEW):
            at = t * 32
            row = (i * NEW + t) * CHUNKS
            att[row : row + CHUNKS, :] = numers[t] / spread_pair(
                denom[:, at : at + 1], denom[:, at + 16 : at + 17], lane
            )
    attended = tiles_to_rows(att, 2 * NEW).astype(bf16)
    out_copy.wait()
    attn_out = jnp.dot(attended, w_out[...], preferred_element_type=f32)
    hidden_one = layer_norm(
        h_zero[at_x] + attn_out, gain_ref[1:2, :], bias_ref[1:2, :]
    ).astype(bf16)
    wait_all(forward_copies())
    total = jnp.zeros((2 * NEW, WIDTH), f32)
    for one in range(SIDE):
        inner = dot_nt(hidden_one, w_ff[0, one])
        inner = (0.5 * inner * (1.0 + lax.erf(inner * math.sqrt(0.5)))).astype(bf16)
        total = total + jnp.dot(inner, w_ff[1, one], preferred_element_type=f32)
    partial[at_y] = total.astype(bf16)
    copies = [
        near_copy(
            partial.at[at_y], partial.at[at_y], y_send.at[k], y_recv.at[k], "seq", y_peer(k)
        )
        for k in range(1, SIDE)
    ]
    start_all(copies)
    wait_all(copies)
    mlp_out = functools.reduce(jnp.add, [partial[k].astype(f32) for k in range(SIDE)])
    final[at_x] = layer_norm(
        hidden_one.astype(f32) + mlp_out, gain_ref[2:3, :], bias_ref[2:3, :]
    ).astype(bf16)
    copies = [
        near_copy(final.at[at_x], final.at[at_x], x_send.at[k], x_recv.at[k], "seq", x_peer(k))
        for k in range(1, SIDE)
    ]
    start_all(copies)
    wait_all(copies)
    for one in range(SIDE):
        rows = final[one].astype(f32)
        for i in range(2):
            out_ref[2 * one + i] = rows[i * NEW : (i + 1) * NEW, :].astype(bf16)


def shards(
    token_ids,
    embed_table,
    ln_gains,
    ln_biases,
    rel_table,
    w_qkv,
    w_out,
    cache_keys,
    cache_values,
    lengths,
    window_starts,
    cache_buckets,
    new_buckets,
    w_in,
    w_down,
):
    slot = (SEQ_N, 2 * CHUNKS, LANES)
    in_vmem = pl.BlockSpec(memory_space=pltpu.VMEM)
    in_smem = pl.BlockSpec(memory_space=pltpu.SMEM)
    in_place = pl.BlockSpec(memory_space=pl.ANY)
    return pl.pallas_call(
        layer_kernel,
        out_shape=jax.ShapeDtypeStruct((GROUP, NEW, WIDTH), bf16),
        in_specs=[
            in_vmem, in_place, in_vmem, in_vmem, in_place, in_place, in_place, in_place, in_place,
            in_smem, in_smem, in_vmem, in_vmem, in_place, in_place,
        ],
        out_specs=in_vmem,
        scratch_shapes=[
            pltpu.VMEM(embed_table.shape, bf16),
            pltpu.VMEM(rel_table.shape, bf16),
            pltpu.VMEM(w_qkv.shape, bf16),
            pltpu.VMEM(w_out.shape, bf16),
            pltpu.VMEM(cache_keys.shape, bf16),
            pltpu.VMEM(cache_values.shape, bf16),
            pltpu.VMEM((2, SIDE) + w_in.shape, bf16),
            pltpu.VMEM((8, LANES), jnp.int32),
            pltpu.VMEM((REQ_N, ROWS, WIDTH), bf16),
            pltpu.VMEM((REQ_N, ROWS, WIDTH), bf16),
            pltpu.VMEM((ROWS * CHUNKS, LANES), f32),
            pltpu.VMEM((1,) + slot, bf16),
            pltpu.VMEM((1,) + slot, bf16),
            pltpu.VMEM((1,) + slot, bf16),
            pltpu.VMEM((SIDE, 2 * NEW, WIDTH), f32),
            pltpu.VMEM((2 * CHUNKS, LANES), f32),
            pltpu.VMEM((2 * NEW * CHUNKS, LANES), f32),
            pltpu.VMEM((GROUP, NEW, 3 * WIDTH), f32),
            pltpu.VMEM((WIDTH, BUCKETS), bf16),
            pltpu.VMEM((BUCKETS, WIDTH), bf16),
            pltpu.VMEM((WIDTH, PIECE), f32),
            pltpu.VMEM((GROUP, PIECE // LANES * NEW * HEADS, LANES), f32),
            pltpu.VMEM((GROUP * NEW * HEADS, WIDTH), bf16),
            pltpu.VMEM((GROUP * NEW * HEADS, BUCKETS), f32),
            pltpu.VMEM((GROUP, NEW * CHUNKS, LANES), bf16),
            pltpu.VMEM((GROUP, CHUNKS, LANES), f32),
            pltpu.VMEM((SEQ_N - 1, 2, NEW * CHUNKS, LANES), bf16),
            pltpu.VMEM((SEQ_N - 1, 2, CHUNKS, LANES), f32),
            pltpu.VMEM((2, NEW * CHUNKS, LANES), f32),
            pltpu.VMEM((2, CHUNKS, LANES), f32),
            pltpu.VMEM((NEW * NEW * CHUNKS, LANES), f32),
            pltpu.VMEM((NEW * CHUNKS, LANES), f32),
            pltpu.VMEM((2 * NEW * NEW, 1), f32),
            pltpu.VMEM((SIDE, 2 * NEW, WIDTH), bf16),
            pltpu.VMEM((SIDE, 2 * NEW, WIDTH), bf16),
            pltpu.SemaphoreType.DMA((8,)),
            pltpu.SemaphoreType.DMA((GROUP,)),
            pltpu.SemaphoreType.DMA((GROUP,)),
        ]
        + [pltpu.SemaphoreType.DMA((REQ_N,))] * 2
        + [pltpu.SemaphoreType.DMA((SEQ_N,))] * 4
        + [pltpu.SemaphoreType.DMA] * 4
        + [pltpu.SemaphoreType.DMA((SIDE,))] * 8,
        compiler_params=pltpu.CompilerParams(
            collective_id=0, has_side_effects=True, vmem_limit_bytes=60 << 20
        ),
        name="decode_layer",
    )(
        token_ids.T, embed_table, ln_gains, ln_biases, rel_table, w_qkv, w_out, cache_keys,
        cache_values, lengths, window_starts, cache_buckets,
        jnp.transpose(new_buckets, (1, 2, 0)), w_in, w_down,
    )


def solution(mesh):
    in_specs = (
        P(),
        P(("req", "seq"), None),
        P(),
        P(),
        P(),
        P(),
        P(),
        P("req", "seq", None),
        P("req", "seq", None),
        P("req"),
        P("req"),
        P("req", None, "seq"),
        P("req", None, None),
        P("seq", None),
        P("seq", None),
    )
    out_specs = P("req", None, None)
    return jax.shard_map(shards, mesh=mesh, in_specs=in_specs, out_specs=out_specs, check_vma=False)
```

```python
import functools
import math

import jax
import jax.numpy as jnp
from jax import lax
from jax.experimental import pallas as pl
from jax.experimental.pallas import tpu as pltpu
from jax.sharding import PartitionSpec as P

HEADS = 16
HEAD_DIM = 64
SINKS = 4
NEW = 4
WIDTH = 1024
REQ_N = 8
SEQ_N = 16
GROUP = 8
ROWS = GROUP * NEW
PIECE = 512
BUCKETS = 512
TILE = 256
LANES = 128
CHUNKS = WIDTH // LANES
SIDE = 4
HOOKS = (3, 5, 7)
FORWARD = 0

norm_epsilon = 1e-06
masked_score = -1e30
score_scale = 1.0 / math.sqrt(3 * HEAD_DIM)
MESH = pl.DeviceIdType.MESH
f32 = jnp.float32
bf16 = jnp.bfloat16


def layer_norm(values, gain, shift):
    center = values - jnp.mean(values, axis=-1, keepdims=True)
    spread = jnp.mean(center * center, axis=-1, keepdims=True)
    return center * lax.rsqrt(spread + norm_epsilon) * gain + shift


def dot_nt(a, b):
    return lax.dot_general(a, b, (((1,), (1,)), ((), ())), preferred_element_type=f32)


def rows_to_tiles(rows, stage, count):
    for c in range(CHUNKS):
        stage[pl.ds(c, count, stride=CHUNKS), :] = rows[:, c * LANES : (c + 1) * LANES]


def tiles_to_rows(stage, count):
    return jnp.concatenate(
        [stage[pl.ds(c, count, stride=CHUNKS), :] for c in range(CHUNKS)], axis=1
    )


def seq_copy(src, dst, send_sem, recv_sem, peer):
    return pltpu.make_async_remote_copy(
        src_ref=src,
        dst_ref=dst,
        send_sem=send_sem,
        recv_sem=recv_sem,
        device_id={"seq": peer},
        device_id_type=MESH,
    )


def seq_scatter(me, send, recv, send_sems, recv_sems):
    copies = []
    for k in range(1, SEQ_N):
        peer = lax.rem(me + k, SEQ_N)
        copy = seq_copy(send.at[peer], recv.at[k], send_sems.at[k], recv_sems.at[k], peer)
        copies.append(copy)
    return copies


def seq_gather(me, buf, send_sems, recv_sems):
    copies = []
    for k in range(1, SEQ_N):
        peer = lax.rem(me + k, SEQ_N)
        copy = seq_copy(buf.at[me], buf.at[me], send_sems.at[k], recv_sems.at[k], peer)
        copies.append(copy)
    return copies


def start_all(copies):
    for copy in copies:
        copy.start()


def wait_all(copies):
    for copy in copies:
        copy.wait()


def spread_pair(column_even, column_odd, lane):
    return jnp.where(lane < HEAD_DIM, column_even, column_odd)


def pack_ml(values, lane):
    out = jnp.zeros((CHUNKS, LANES), f32)
    for g, value in enumerate(values):
        out = jnp.where((lane >> 3) == g, value, out)
    return out


def layer_kernel(
    ids_ref, table_hbm, gain_ref, bias_ref, rel_hbm, w_hbm, w_out_hbm, keys_hbm, values_hbm,
    lengths_ref, starts_ref, buckets_ref, new_ref, w_in_hbm, w_down_hbm,
    out_ref,
    table, rel, w_qkv, w_out, keys, values, w_ff, ids_pad,
    send, land, stage, tiles, got, hid, h_zero, rows_f, att, proj, pos_lhs, pos_key, keys_t,
    from_pos, queries, q_table, msg_numer, msg_ml, in_numer, in_ml, fresh_numer, fresh_ml,
    fresh_stage, v_stage, picks, partial, final,
    local_sems, key_sems, value_sems,
    req_send, req_recv, rs_send, rs_recv, ag_send, ag_recv,
    n_send, n_recv, m_send, m_recv, w_send, w_recv, f_send, f_recv, y_send, y_recv, x_send, x_recv,
):
    me = lax.axis_index("seq")
    req = lax.axis_index("req")
    at_x, at_y = me // SIDE, lax.rem(me, SIDE)
    core = lax.rem(req, 2)
    table_rows = NEW * HEADS
    lane = lax.broadcasted_iota(jnp.int32, (CHUNKS, LANES), 1)

    def local(src, dst, index):
        return pltpu.make_async_copy(src, dst, local_sems.at[index])

    table_copy = local(table_hbm, table, 0)
    rel_copy = local(rel_hbm, rel, 1)
    w_copies = [
        local(
            w_hbm.at[:, i * WIDTH : (i + 1) * WIDTH], w_qkv.at[:, i * WIDTH : (i + 1) * WIDTH], 2 + i
        )
        for i in range(3)
    ]
    out_copy = local(w_out_hbm, w_out, 5)
    in_copy = local(w_in_hbm, w_ff.at[0, at_x], 6)
    down_copy = local(w_down_hbm, w_ff.at[1, at_x], 7)

    def key_copy(r):
        return pltpu.make_async_copy(keys_hbm.at[r], keys.at[r], key_sems.at[r])

    def value_copy(r):
        return pltpu.make_async_copy(values_hbm.at[r], values.at[r], value_sems.at[r])

    table_copy.start()
    rel_copy.start()
    w_copies[0].start()
    w_copies[1].start()
    barrier = pltpu.get_barrier_semaphore()
    for k in range(1, SEQ_N):
        pl.semaphore_signal(
            barrier, inc=1, device_id={"seq": lax.rem(me + k, SEQ_N)}, device_id_type=MESH
        )
    for k in range(1, REQ_N):
        pl.semaphore_signal(
            barrier, inc=1, device_id={"req": lax.rem(req + k, REQ_N)}, device_id_type=MESH
        )
    key_copy(0).start()
    in_copy.start()
    down_copy.start()

    vocab_rows = table.shape[0]
    ids_pad[...] = jnp.zeros((8, LANES), jnp.int32)
    ids_pad[0:NEW, 0 : REQ_N * GROUP] = ids_ref[...]
    ids_t = ids_pad[...].T
    ids = jnp.concatenate(
        [
            ids_t[g * GROUP : (g + 1) * GROUP, t : t + 1]
            for g in range(REQ_N)
            for t in range(NEW)
        ],
        axis=0,
    ) - (req * SEQ_N + me) * vocab_rows
    one_hot = (
        lax.broadcasted_iota(jnp.int32, (REQ_N * ROWS, vocab_rows), 1) == ids
    ).astype(f32).astype(bf16)
    table_copy.wait()
    send[...] = (
        jnp.dot(one_hot, table[...], preferred_element_type=f32)
        .astype(bf16)
        .reshape(REQ_N, ROWS, WIDTH)
    )
    pl.semaphore_wait(barrier, SEQ_N - 1 + REQ_N - 1)

    def req_copies():
        copies = []
        for k in range(1, REQ_N):
            peer = lax.rem(req + k, REQ_N)
            copies.append(
                pltpu.make_async_remote_copy(
                    src_ref=send.at[peer],
                    dst_ref=land.at[k],
                    send_sem=req_send.at[k],
                    recv_sem=req_recv.at[k],
                    device_id={"req": peer},
                    device_id_type=MESH,
                )
            )
        return copies

    for copy in req_copies():
        copy.start()

    def near_copy(src, dst, send_sem, recv_sem, axis, peer):
        return pltpu.make_async_remote_copy(
            src_ref=src,
            dst_ref=dst,
            send_sem=send_sem,
            recv_sem=recv_sem,
            device_id={axis: peer},
            device_id_type=MESH,
        )

    def x_slot(k):
        return lax.rem(at_x + k, SIDE)

    def x_peer(k):
        return x_slot(k) * SIDE + at_y

    def y_peer(k):
        return at_x * SIDE + lax.rem(at_y + k, SIDE)

    def shard_copies():
        held = w_ff.at[core, at_x]
        return [
            near_copy(held, held, w_send.at[k], w_recv.at[k], "seq", x_peer(k)) for k in (1, 3)
        ]

    def far_copies():
        half = w_ff.shape[2] // 2
        copies = []
        for index, (k, rows) in enumerate(((1, slice(0, half)), (3, slice(half, 2 * half)))):
            held = w_ff.at[core, x_slot(k + 2), rows]
            copies.append(
                near_copy(held, held, w_send.at[2 * index], w_recv.at[2 * index], "seq", x_peer(k))
            )
        return copies

    def forward_copies(offsets):
        copies = []
        for k in offsets:
            held = w_ff.at[core, x_slot(k)]
            copies.append(
                near_copy(held, held, f_send.at[k], f_recv.at[k], "req", req + 1 - 2 * core)
            )
        return copies

    in_copy.wait()
    down_copy.wait()
    start_all(shard_copies())

    rel_copy.wait()
    relative = layer_norm(rel[...].astype(f32), gain_ref[3:4, :], bias_ref[3:4, :]).astype(bf16)
    flip = (
        lax.broadcasted_iota(jnp.int32, (BUCKETS, BUCKETS), 0)
        + lax.broadcasted_iota(jnp.int32, (BUCKETS, BUCKETS), 1)
        == BUCKETS - 1
    ).astype(f32).astype(bf16)
    flipped = jnp.dot(flip, relative, preferred_element_type=f32).astype(bf16)
    w_copies[0].wait()
    pos_lhs[...] = (
        jnp.dot(flipped, w_qkv[:, 0:WIDTH], preferred_element_type=f32).astype(bf16).T
    )
    w_copies[1].wait()
    key_copy(1).start()
    w_copies[2].start()
    pos_key[...] = jnp.dot(
        relative, w_qkv[:, WIDTH : 2 * WIDTH], preferred_element_type=f32
    ).astype(bf16)

    def own_head():
        row = lax.broadcasted_iota(jnp.int32, (NEW, HEADS, WIDTH), 1)
        col_head = lax.broadcasted_iota(jnp.int32, (NEW, HEADS, WIDTH), 2) >> 6
        return 2 * (row & (CHUNKS - 1)) + (row >> 3) == col_head

    def from_pos_step(r, carry):
        value_copy(r).start()

        @pl.when(r < GROUP - 2)
        def _():
            key_copy(r + 2).start()

        @pl.when(r == 0)
        def _():
            out_copy.start()

        @pl.when(r == HOOKS[0])
        def _():
            copies = req_copies()
            total = send[req].astype(f32)
            for k in range(1, REQ_N):
                copies[k - 1].wait()
                total = total + land[k].astype(f32)
            for t in range(NEW):
                for c in range(CHUNKS):
                    stage[pl.ds(t * CHUNKS + c, GROUP, stride=NEW * CHUNKS), :] = total[
                        t * GROUP : (t + 1) * GROUP, c * LANES : (c + 1) * LANES
                    ]
            tiles[0] = stage[...].reshape(SEQ_N, 2 * CHUNKS, LANES).astype(bf16)
            start_all(seq_scatter(me, tiles.at[0], got.at[0], rs_send, rs_recv))

        @pl.when(r == HOOKS[1])
        def _():
            copies = seq_scatter(me, tiles.at[0], got.at[0], rs_send, rs_recv)
            own = tiles[0, me].astype(f32)
            for k in range(1, SEQ_N):
                copies[k - 1].wait()
                own = own + got[0, k].astype(f32)
            rows_f[...] = own
            hidden = layer_norm(tiles_to_rows(rows_f, 2), gain_ref[0:1, :], bias_ref[0:1, :])
            rows_to_tiles(hidden, rows_f, 2)
            hid[0, me] = rows_f[...].astype(bf16)
            start_all(seq_gather(me, hid.at[0], ag_send, ag_recv))

        @pl.when(r == HOOKS[2])
        def _():
            wait_all(seq_gather(me, hid.at[0], ag_send, ag_recv))
            stage[...] = hid[0].astype(f32).reshape(ROWS * CHUNKS, LANES)
            hidden = tiles_to_rows(stage, ROWS)
            for one in range(SIDE):
                h_zero[one] = hidden[one * 2 * NEW : (one + 1) * 2 * NEW, :]
            hidden = hidden.astype(bf16)
            w_copies[2].wait()
            projected = (
                jnp.dot(hidden, w_qkv[...], preferred_element_type=f32).astype(bf16).astype(f32)
            )
            mine = own_head()
            for one in range(GROUP):
                block = projected[one * NEW : (one + 1) * NEW, :]
                proj[one] = block
                q_all = jnp.broadcast_to(block[:, None, 0:WIDTH], (NEW, HEADS, WIDTH))
                queries[one * table_rows : (one + 1) * table_rows, :] = (
                    jnp.where(mine, q_all, 0.0).reshape(table_rows, WIDTH).astype(bf16)
                )
            q_table[...] = dot_nt(queries[...], pos_key[...])

        key_copy(r).wait()
        keys_t[...] = keys[r].T.astype(f32)
        for t in range(NEW):
            for half in range(PIECE // TILE):
                cols = slice(half * TILE, (half + 1) * TILE)
                chosen = (
                    lax.broadcasted_iota(jnp.int32, (BUCKETS, TILE), 0)
                    == buckets_ref[r, t : t + 1, cols]
                ).astype(f32).astype(bf16)
                product = (
                    jnp.dot(pos_lhs[...], chosen, preferred_element_type=f32) * keys_t[:, cols]
                )
                heads_sum = jnp.sum(product.reshape(HEADS, HEAD_DIM, TILE), axis=1)
                for sub in range(TILE // LANES):
                    at = (half * (TILE // LANES) + sub) * table_rows + t * HEADS
                    from_pos[r, at : at + HEADS, :] = heads_sum[
                        :, sub * LANES : (sub + 1) * LANES
                    ]
        return carry

    lax.fori_loop(0, GROUP, from_pos_step, 0)

    first = me * PIECE

    def message_copies(r, k):
        peer = (r // 2) * SIDE + k
        slot = lax.rem(peer - me + SEQ_N, SEQ_N) - 1
        part = lax.rem(r, 2)
        return peer, [
            near_copy(msg_numer.at[r], in_numer.at[slot, part], n_send, n_recv, "seq", peer),
            near_copy(msg_ml.at[r], in_ml.at[slot, part], m_send, m_recv, "seq", peer),
        ]

    def attend_step(r, carry):
        @pl.when(r == FORWARD)
        def _():
            wait_all(shard_copies())
            start_all(far_copies())
            start_all(forward_copies((1, 3)))

        value_copy(r).wait()
        span = pl.ds(pl.multiple_of(r * table_rows, table_rows), table_rows)
        content = dot_nt(queries[span, :], keys[r])
        parts = []
        for t in range(NEW):
            tables = [
                q_table[
                    pl.ds(pl.multiple_of(r * table_rows + t * HEADS, HEADS), HEADS),
                    kb * LANES : (kb + 1) * LANES,
                ]
                for kb in range(BUCKETS // LANES)
            ]
            columns = []
            for sub in range(PIECE // LANES):
                bucket = jnp.broadcast_to(
                    buckets_ref[r, t : t + 1, sub * LANES : (sub + 1) * LANES], (HEADS, LANES)
                )
                low = bucket & (LANES - 1)
                high = bucket >> 7
                picked = jnp.take_along_axis(tables[0], low, axis=1)
                for kb in range(1, BUCKETS // LANES):
                    picked = jnp.where(
                        high == kb, jnp.take_along_axis(tables[kb], low, axis=1), picked
                    )
                back = jnp.concatenate(
                    [
                        from_pos[
                            r, pl.ds(sub * table_rows + t * HEADS + j, CHUNKS, stride=2), :
                        ]
                        for j in range(2)
                    ],
                    axis=0,
                )
                columns.append(picked + back)
            parts.append(jnp.concatenate(columns, axis=1))
        total = content + jnp.concatenate(parts, axis=0)
        position = first + lax.broadcasted_iota(jnp.int32, (table_rows, PIECE), 1)
        allowed = (position < lengths_ref[r]) & (
            (position < SINKS) | (position >= starts_ref[r])
        )
        scores = jnp.where(allowed, total * score_scale, masked_score)
        top = jnp.max(scores, axis=1, keepdims=True)
        weights = jnp.where(allowed, jnp.exp(scores - top), 0.0)
        sums = jnp.sum(weights, axis=1, keepdims=True)
        wide = jnp.dot(weights.astype(bf16), values[r], preferred_element_type=f32)
        numer = jnp.sum(jnp.where(own_head(), wide.reshape(NEW, HEADS, WIDTH), 0.0), axis=1)
        rows_to_tiles(numer, v_stage, NEW)
        msg_numer[r] = v_stage[0 : NEW * CHUNKS, :].astype(bf16)
        columns = []
        for token in range(NEW):
            for j in range(2):
                at = token * HEADS + j * CHUNKS
                columns.append(top[at : at + CHUNKS])
                columns.append(sums[at : at + CHUNKS])
        msg_ml[r] = pack_ml(columns, lane)
        for k in range(SIDE):
            peer, copies = message_copies(r, k)

            @pl.when(peer != me)
            def _():
                start_all(copies)

        return carry

    lax.fori_loop(0, GROUP, attend_step, 0)

    wait_all(far_copies())
    start_all(forward_copies((2,)))

    new_lane = lax.broadcasted_iota(jnp.int32, (NEW, NEW, GROUP), 2)
    new_all = new_ref[...].astype(f32)
    for i in range(2):
        wanted = jnp.sum(
            jnp.where(new_lane == 2 * at_x + i, new_all, 0.0), axis=2, keepdims=True
        )
        for t in range(NEW):
            at = (i * NEW + t) * NEW
            picks[at : at + NEW, :] = wanted[t]
    picked = (
        lax.broadcasted_iota(jnp.int32, (2 * NEW * NEW, BUCKETS), 1).astype(f32) == picks[...]
    ).astype(f32).astype(bf16)
    pq = dot_nt(picked, pos_lhs[...])
    pk = jnp.dot(picked, pos_key[...], preferred_element_type=f32)
    for i in range(2):
        mine = proj[2 * at_x + i]
        q4, k4, v4 = (mine[:, w * WIDTH : (w + 1) * WIDTH] for w in range(3))
        pairs = NEW * NEW
        q16 = jnp.broadcast_to(q4[:, None, :], (NEW, NEW, WIDTH)).reshape(pairs, WIDTH)
        k16 = jnp.broadcast_to(k4[None], (NEW, NEW, WIDTH)).reshape(pairs, WIDTH)
        span = slice(i * pairs, (i + 1) * pairs)
        rows_to_tiles(q16 * (k16 + pk[span]) + k16 * pq[span], fresh_stage, pairs)
        rows_to_tiles(v4, v_stage, NEW)
        columns = []
        for t in range(NEW):
            spread = []
            for u in range(t + 1):
                at = (t * NEW + u) * CHUNKS
                terms = fresh_stage[at : at + CHUNKS, :]
                even = jnp.sum(jnp.where(lane < HEAD_DIM, terms, 0.0), axis=1, keepdims=True)
                other = jnp.sum(jnp.where(lane >= HEAD_DIM, terms, 0.0), axis=1, keepdims=True)
                spread.append(spread_pair(even, other, lane) * score_scale)
            top = functools.reduce(jnp.maximum, spread)
            sums = jnp.zeros_like(top)
            numer = jnp.zeros_like(top)
            for u in range(t + 1):
                weight = jnp.exp(spread[u] - top)
                sums = sums + weight
                numer = numer + weight.astype(bf16).astype(f32) * v_stage[
                    u * CHUNKS : (u + 1) * CHUNKS, :
                ]
            fresh_numer[i, t * CHUNKS : (t + 1) * CHUNKS, :] = numer
            for at in (0, HEAD_DIM):
                columns.append(top[:, at : at + 1])
                columns.append(sums[:, at : at + 1])
        fresh_ml[i] = pack_ml(columns, lane)

    near_copy(in_numer, in_numer, n_send, n_recv, "seq", x_peer(1)).wait()
    near_copy(in_ml, in_ml, m_send, m_recv, "seq", x_peer(1)).wait()
    for i in range(2):
        mls = [in_ml[k, i] for k in range(SEQ_N - 1)] + [msg_ml[2 * at_x + i], fresh_ml[i]]
        top = functools.reduce(jnp.maximum, mls)
        factors = [jnp.exp(ml - top) for ml in mls]
        denom = functools.reduce(
            jnp.add, [f * pltpu.roll(ml, LANES - 8, axis=1) for f, ml in zip(factors, mls)]
        )
        numers = [jnp.zeros((CHUNKS, LANES), f32) for _ in range(NEW)]
        for k, factor in enumerate(factors):
            if k < SEQ_N - 1:
                block = in_numer[k, i].astype(f32)
            elif k == SEQ_N - 1:
                block = msg_numer[2 * at_x + i].astype(f32)
            else:
                block = fresh_numer[i]
            for t in range(NEW):
                at = t * 32
                numers[t] = numers[t] + block[t * CHUNKS : (t + 1) * CHUNKS] * spread_pair(
                    factor[:, at : at + 1], factor[:, at + 16 : at + 17], lane
                )
        for t in range(NEW):
            at = t * 32
            row = (i * NEW + t) * CHUNKS
            att[row : row + CHUNKS, :] = numers[t] / spread_pair(
                denom[:, at : at + 1], denom[:, at + 16 : at + 17], lane
            )
    attended = tiles_to_rows(att, 2 * NEW).astype(bf16)
    out_copy.wait()
    attn_out = jnp.dot(attended, w_out[...], preferred_element_type=f32)
    hidden_one = layer_norm(
        h_zero[at_x] + attn_out, gain_ref[1:2, :], bias_ref[1:2, :]
    ).astype(bf16)
    wait_all(forward_copies((1, 2, 3)))
    total = jnp.zeros((2 * NEW, WIDTH), f32)
    for one in range(SIDE):
        inner = dot_nt(hidden_one, w_ff[0, one])
        inner = (0.5 * inner * (1.0 + lax.erf(inner * math.sqrt(0.5)))).astype(bf16)
        total = total + jnp.dot(inner, w_ff[1, one], preferred_element_type=f32)
    partial[at_y] = total.astype(bf16)
    copies = [
        near_copy(
            partial.at[at_y], partial.at[at_y], y_send.at[k], y_recv.at[k], "seq", y_peer(k)
        )
        for k in range(1, SIDE)
    ]
    start_all(copies)
    wait_all(copies)
    mlp_out = functools.reduce(jnp.add, [partial[k].astype(f32) for k in range(SIDE)])
    final[at_x] = layer_norm(
        hidden_one.astype(f32) + mlp_out, gain_ref[2:3, :], bias_ref[2:3, :]
    ).astype(bf16)
    copies = [
        near_copy(final.at[at_x], final.at[at_x], x_send.at[k], x_recv.at[k], "seq", x_peer(k))
        for k in range(1, SIDE)
    ]
    start_all(copies)
    wait_all(copies)
    for one in range(SIDE):
        rows = final[one].astype(f32)
        for i in range(2):
            out_ref[2 * one + i] = rows[i * NEW : (i + 1) * NEW, :].astype(bf16)


def shards(
    token_ids,
    embed_table,
    ln_gains,
    ln_biases,
    rel_table,
    w_qkv,
    w_out,
    cache_keys,
    cache_values,
    lengths,
    window_starts,
    cache_buckets,
    new_buckets,
    w_in,
    w_down,
):
    slot = (SEQ_N, 2 * CHUNKS, LANES)
    in_vmem = pl.BlockSpec(memory_space=pltpu.VMEM)
    in_smem = pl.BlockSpec(memory_space=pltpu.SMEM)
    in_place = pl.BlockSpec(memory_space=pl.ANY)
    return pl.pallas_call(
        layer_kernel,
        out_shape=jax.ShapeDtypeStruct((GROUP, NEW, WIDTH), bf16),
        in_specs=[
            in_vmem, in_place, in_vmem, in_vmem, in_place, in_place, in_place, in_place, in_place,
            in_smem, in_smem, in_vmem, in_vmem, in_place, in_place,
        ],
        out_specs=in_vmem,
        scratch_shapes=[
            pltpu.VMEM(embed_table.shape, bf16),
            pltpu.VMEM(rel_table.shape, bf16),
            pltpu.VMEM(w_qkv.shape, bf16),
            pltpu.VMEM(w_out.shape, bf16),
            pltpu.VMEM(cache_keys.shape, bf16),
            pltpu.VMEM(cache_values.shape, bf16),
            pltpu.VMEM((2, SIDE) + w_in.shape, bf16),
            pltpu.VMEM((8, LANES), jnp.int32),
            pltpu.VMEM((REQ_N, ROWS, WIDTH), bf16),
            pltpu.VMEM((REQ_N, ROWS, WIDTH), bf16),
            pltpu.VMEM((ROWS * CHUNKS, LANES), f32),
            pltpu.VMEM((1,) + slot, bf16),
            pltpu.VMEM((1,) + slot, bf16),
            pltpu.VMEM((1,) + slot, bf16),
            pltpu.VMEM((SIDE, 2 * NEW, WIDTH), f32),
            pltpu.VMEM((2 * CHUNKS, LANES), f32),
            pltpu.VMEM((2 * NEW * CHUNKS, LANES), f32),
            pltpu.VMEM((GROUP, NEW, 3 * WIDTH), f32),
            pltpu.VMEM((WIDTH, BUCKETS), bf16),
            pltpu.VMEM((BUCKETS, WIDTH), bf16),
            pltpu.VMEM((WIDTH, PIECE), f32),
            pltpu.VMEM((GROUP, PIECE // LANES * NEW * HEADS, LANES), f32),
            pltpu.VMEM((GROUP * NEW * HEADS, WIDTH), bf16),
            pltpu.VMEM((GROUP * NEW * HEADS, BUCKETS), f32),
            pltpu.VMEM((GROUP, NEW * CHUNKS, LANES), bf16),
            pltpu.VMEM((GROUP, CHUNKS, LANES), f32),
            pltpu.VMEM((SEQ_N - 1, 2, NEW * CHUNKS, LANES), bf16),
            pltpu.VMEM((SEQ_N - 1, 2, CHUNKS, LANES), f32),
            pltpu.VMEM((2, NEW * CHUNKS, LANES), f32),
            pltpu.VMEM((2, CHUNKS, LANES), f32),
            pltpu.VMEM((NEW * NEW * CHUNKS, LANES), f32),
            pltpu.VMEM((NEW * CHUNKS, LANES), f32),
            pltpu.VMEM((2 * NEW * NEW, 1), f32),
            pltpu.VMEM((SIDE, 2 * NEW, WIDTH), bf16),
            pltpu.VMEM((SIDE, 2 * NEW, WIDTH), bf16),
            pltpu.SemaphoreType.DMA((8,)),
            pltpu.SemaphoreType.DMA((GROUP,)),
            pltpu.SemaphoreType.DMA((GROUP,)),
        ]
        + [pltpu.SemaphoreType.DMA((REQ_N,))] * 2
        + [pltpu.SemaphoreType.DMA((SEQ_N,))] * 4
        + [pltpu.SemaphoreType.DMA] * 4
        + [pltpu.SemaphoreType.DMA((SIDE,))] * 8,
        compiler_params=pltpu.CompilerParams(
            collective_id=0, has_side_effects=True, vmem_limit_bytes=60 << 20
        ),
        name="decode_layer",
    )(
        token_ids.T, embed_table, ln_gains, ln_biases, rel_table, w_qkv, w_out, cache_keys,
        cache_values, lengths, window_starts, cache_buckets,
        jnp.transpose(new_buckets, (1, 2, 0)), w_in, w_down,
    )


def solution(mesh):
    in_specs = (
        P(),
        P(("req", "seq"), None),
        P(),
        P(),
        P(),
        P(),
        P(),
        P("req", "seq", None),
        P("req", "seq", None),
        P("req"),
        P("req"),
        P("req", None, "seq"),
        P("req", None, None),
        P("seq", None),
        P("seq", None),
    )
    out_specs = P("req", None, None)
    return jax.shard_map(shards, mesh=mesh, in_specs=in_specs, out_specs=out_specs, check_vma=False)
```

```python
import functools
import math

import jax
import jax.numpy as jnp
from jax import lax
from jax.experimental import pallas as pl
from jax.experimental.pallas import tpu as pltpu
from jax.sharding import PartitionSpec as P

HEADS = 16
HEAD_DIM = 64
SINKS = 4
NEW = 4
WIDTH = 1024
REQ_N = 8
SEQ_N = 16
GROUP = 8
ROWS = GROUP * NEW
PIECE = 512
BUCKETS = 512
TILE = 256
LANES = 128
CHUNKS = WIDTH // LANES
SIDE = 4
HOOKS = (3, 5, 7)
PASS_ON = 6
FORWARD = 6

norm_epsilon = 1e-06
masked_score = -1e30
score_scale = 1.0 / math.sqrt(3 * HEAD_DIM)
MESH = pl.DeviceIdType.MESH
f32 = jnp.float32
bf16 = jnp.bfloat16


def layer_norm(values, gain, shift):
    center = values - jnp.mean(values, axis=-1, keepdims=True)
    spread = jnp.mean(center * center, axis=-1, keepdims=True)
    return center * lax.rsqrt(spread + norm_epsilon) * gain + shift


def dot_nt(a, b):
    return lax.dot_general(a, b, (((1,), (1,)), ((), ())), preferred_element_type=f32)


def rows_to_tiles(rows, stage, count):
    for c in range(CHUNKS):
        stage[pl.ds(c, count, stride=CHUNKS), :] = rows[:, c * LANES : (c + 1) * LANES]


def tiles_to_rows(stage, count):
    return jnp.concatenate(
        [stage[pl.ds(c, count, stride=CHUNKS), :] for c in range(CHUNKS)], axis=1
    )


def seq_copy(src, dst, send_sem, recv_sem, peer):
    return pltpu.make_async_remote_copy(
        src_ref=src,
        dst_ref=dst,
        send_sem=send_sem,
        recv_sem=recv_sem,
        device_id={"seq": peer},
        device_id_type=MESH,
    )


def seq_scatter(me, send, recv, send_sems, recv_sems):
    copies = []
    for k in range(1, SEQ_N):
        peer = lax.rem(me + k, SEQ_N)
        copy = seq_copy(send.at[peer], recv.at[k], send_sems.at[k], recv_sems.at[k], peer)
        copies.append(copy)
    return copies


def seq_gather(me, buf, send_sems, recv_sems):
    copies = []
    for k in range(1, SEQ_N):
        peer = lax.rem(me + k, SEQ_N)
        copy = seq_copy(buf.at[me], buf.at[me], send_sems.at[k], recv_sems.at[k], peer)
        copies.append(copy)
    return copies


def start_all(copies):
    for copy in copies:
        copy.start()


def wait_all(copies):
    for copy in copies:
        copy.wait()


def spread_pair(column_even, column_odd, lane):
    return jnp.where(lane < HEAD_DIM, column_even, column_odd)


def pack_ml(values, lane):
    out = jnp.zeros((CHUNKS, LANES), f32)
    for g, value in enumerate(values):
        out = jnp.where((lane >> 3) == g, value, out)
    return out


def layer_kernel(
    ids_ref, table_hbm, gain_ref, bias_ref, rel_hbm, w_hbm, w_out_hbm, keys_hbm, values_hbm,
    lengths_ref, starts_ref, buckets_ref, new_ref, w_in_hbm, w_down_hbm,
    out_ref,
    table, rel, w_qkv, w_out, keys, values, w_ff, ids_pad,
    send, land, stage, tiles, got, hid, h_zero, rows_f, att, proj, pos_lhs, pos_key, keys_t,
    from_pos, queries, q_table, msg_numer, msg_ml, in_numer, in_ml, fresh_numer, fresh_ml,
    fresh_stage, v_stage, picks, partial, final,
    local_sems, key_sems, value_sems,
    req_send, req_recv, rs_send, rs_recv, ag_send, ag_recv,
    n_send, n_recv, m_send, m_recv, w_send, w_recv, f_send, f_recv, y_send, y_recv, x_send, x_recv,
):
    me = lax.axis_index("seq")
    req = lax.axis_index("req")
    at_x, at_y = me // SIDE, lax.rem(me, SIDE)
    core = lax.rem(req, 2)
    table_rows = NEW * HEADS
    lane = lax.broadcasted_iota(jnp.int32, (CHUNKS, LANES), 1)

    def local(src, dst, index):
        return pltpu.make_async_copy(src, dst, local_sems.at[index])

    table_copy = local(table_hbm, table, 0)
    rel_copy = local(rel_hbm, rel, 1)
    w_copies = [
        local(
            w_hbm.at[:, i * WIDTH : (i + 1) * WIDTH], w_qkv.at[:, i * WIDTH : (i + 1) * WIDTH], 2 + i
        )
        for i in range(3)
    ]
    out_copy = local(w_out_hbm, w_out, 5)
    in_copy = local(w_in_hbm, w_ff.at[0, at_x], 6)
    down_copy = local(w_down_hbm, w_ff.at[1, at_x], 7)

    def key_copy(r):
        return pltpu.make_async_copy(keys_hbm.at[r], keys.at[r], key_sems.at[r])

    def value_copy(r):
        return pltpu.make_async_copy(values_hbm.at[r], values.at[r], value_sems.at[r])

    table_copy.start()
    rel_copy.start()
    w_copies[0].start()
    w_copies[1].start()
    barrier = pltpu.get_barrier_semaphore()
    for k in range(1, SEQ_N):
        pl.semaphore_signal(
            barrier, inc=1, device_id={"seq": lax.rem(me + k, SEQ_N)}, device_id_type=MESH
        )
    for k in range(1, REQ_N):
        pl.semaphore_signal(
            barrier, inc=1, device_id={"req": lax.rem(req + k, REQ_N)}, device_id_type=MESH
        )
    key_copy(0).start()
    in_copy.start()
    down_copy.start()

    vocab_rows = table.shape[0]
    ids_pad[...] = jnp.zeros((8, LANES), jnp.int32)
    ids_pad[0:NEW, 0 : REQ_N * GROUP] = ids_ref[...]
    ids_t = ids_pad[...].T
    ids = jnp.concatenate(
        [
            ids_t[g * GROUP : (g + 1) * GROUP, t : t + 1]
            for g in range(REQ_N)
            for t in range(NEW)
        ],
        axis=0,
    ) - (req * SEQ_N + me) * vocab_rows
    one_hot = (
        lax.broadcasted_iota(jnp.int32, (REQ_N * ROWS, vocab_rows), 1) == ids
    ).astype(f32).astype(bf16)
    table_copy.wait()
    send[...] = (
        jnp.dot(one_hot, table[...], preferred_element_type=f32)
        .astype(bf16)
        .reshape(REQ_N, ROWS, WIDTH)
    )
    rel_copy.wait()
    relative = layer_norm(rel[...].astype(f32), gain_ref[3:4, :], bias_ref[3:4, :]).astype(bf16)
    flip = (
        lax.broadcasted_iota(jnp.int32, (BUCKETS, BUCKETS), 0)
        + lax.broadcasted_iota(jnp.int32, (BUCKETS, BUCKETS), 1)
        == BUCKETS - 1
    ).astype(f32).astype(bf16)
    flipped = jnp.dot(flip, relative, preferred_element_type=f32).astype(bf16)
    pl.semaphore_wait(barrier, SEQ_N - 1 + REQ_N - 1)

    def req_copies():
        copies = []
        for k in range(1, REQ_N):
            peer = lax.rem(req + k, REQ_N)
            copies.append(
                pltpu.make_async_remote_copy(
                    src_ref=send.at[peer],
                    dst_ref=land.at[k],
                    send_sem=req_send.at[k],
                    recv_sem=req_recv.at[k],
                    device_id={"req": peer},
                    device_id_type=MESH,
                )
            )
        return copies

    for copy in req_copies():
        copy.start()

    def near_copy(src, dst, send_sem, recv_sem, axis, peer):
        return pltpu.make_async_remote_copy(
            src_ref=src,
            dst_ref=dst,
            send_sem=send_sem,
            recv_sem=recv_sem,
            device_id={axis: peer},
            device_id_type=MESH,
        )

    def x_slot(k):
        return lax.rem(at_x + k, SIDE)

    def x_peer(k):
        return x_slot(k) * SIDE + at_y

    def y_peer(k):
        return at_x * SIDE + lax.rem(at_y + k, SIDE)

    def shard_copies():
        held = w_ff.at[core, at_x]
        return [
            near_copy(held, held, w_send.at[k], w_recv.at[k], "seq", x_peer(k)) for k in (1, 3)
        ]

    def far_copies():
        half = w_ff.shape[2] // 2
        copies = []
        for index, (k, rows) in enumerate(((1, slice(0, half)), (3, slice(half, 2 * half)))):
            held = w_ff.at[core, x_slot(k + 2), rows]
            copies.append(
                near_copy(held, held, w_send.at[2 * index], w_recv.at[2 * index], "seq", x_peer(k))
            )
        return copies

    def forward_copies(offsets):
        copies = []
        for k in offsets:
            held = w_ff.at[core, x_slot(k)]
            copies.append(
                near_copy(held, held, f_send.at[k], f_recv.at[k], "req", req + 1 - 2 * core)
            )
        return copies

    in_copy.wait()
    down_copy.wait()
    start_all(shard_copies())

    w_copies[0].wait()
    pos_lhs[...] = (
        jnp.dot(flipped, w_qkv[:, 0:WIDTH], preferred_element_type=f32).astype(bf16).T
    )
    w_copies[1].wait()
    key_copy(1).start()
    w_copies[2].start()
    pos_key[...] = jnp.dot(
        relative, w_qkv[:, WIDTH : 2 * WIDTH], preferred_element_type=f32
    ).astype(bf16)

    def own_head():
        row = lax.broadcasted_iota(jnp.int32, (NEW, HEADS, WIDTH), 1)
        col_head = lax.broadcasted_iota(jnp.int32, (NEW, HEADS, WIDTH), 2) >> 6
        return 2 * (row & (CHUNKS - 1)) + (row >> 3) == col_head

    def from_pos_step(r, carry):
        value_copy(r).start()

        @pl.when(r < GROUP - 2)
        def _():
            key_copy(r + 2).start()

        @pl.when(r == 0)
        def _():
            out_copy.start()

        @pl.when(r == PASS_ON)
        def _():
            wait_all(shard_copies())
            start_all(far_copies())
            start_all(forward_copies((1, 3)))

        @pl.when(r == HOOKS[0])
        def _():
            copies = req_copies()
            total = send[req].astype(f32)
            for k in range(1, REQ_N):
                copies[k - 1].wait()
                total = total + land[k].astype(f32)
            for t in range(NEW):
                for c in range(CHUNKS):
                    stage[pl.ds(t * CHUNKS + c, GROUP, stride=NEW * CHUNKS), :] = total[
                        t * GROUP : (t + 1) * GROUP, c * LANES : (c + 1) * LANES
                    ]
            tiles[0] = stage[...].reshape(SEQ_N, 2 * CHUNKS, LANES).astype(bf16)
            start_all(seq_scatter(me, tiles.at[0], got.at[0], rs_send, rs_recv))

        @pl.when(r == HOOKS[1])
        def _():
            copies = seq_scatter(me, tiles.at[0], got.at[0], rs_send, rs_recv)
            own = tiles[0, me].astype(f32)
            for k in range(1, SEQ_N):
                copies[k - 1].wait()
                own = own + got[0, k].astype(f32)
            rows_f[...] = own
            hidden = layer_norm(tiles_to_rows(rows_f, 2), gain_ref[0:1, :], bias_ref[0:1, :])
            rows_to_tiles(hidden, rows_f, 2)
            hid[0, me] = rows_f[...].astype(bf16)
            start_all(seq_gather(me, hid.at[0], ag_send, ag_recv))

        @pl.when(r == HOOKS[2])
        def _():
            wait_all(seq_gather(me, hid.at[0], ag_send, ag_recv))
            stage[...] = hid[0].astype(f32).reshape(ROWS * CHUNKS, LANES)
            hidden = tiles_to_rows(stage, ROWS)
            for one in range(SIDE):
                h_zero[one] = hidden[one * 2 * NEW : (one + 1) * 2 * NEW, :]
            hidden = hidden.astype(bf16)
            w_copies[2].wait()
            projected = (
                jnp.dot(hidden, w_qkv[...], preferred_element_type=f32).astype(bf16).astype(f32)
            )
            mine = own_head()
            for one in range(GROUP):
                block = projected[one * NEW : (one + 1) * NEW, :]
                proj[one] = block
                q_all = jnp.broadcast_to(block[:, None, 0:WIDTH], (NEW, HEADS, WIDTH))
                queries[one * table_rows : (one + 1) * table_rows, :] = (
                    jnp.where(mine, q_all, 0.0).reshape(table_rows, WIDTH).astype(bf16)
                )
            q_table[...] = dot_nt(queries[...], pos_key[...])

        key_copy(r).wait()
        keys_t[...] = keys[r].T.astype(f32)
        for t in range(NEW):
            for half in range(PIECE // TILE):
                cols = slice(half * TILE, (half + 1) * TILE)
                chosen = (
                    lax.broadcasted_iota(jnp.int32, (BUCKETS, TILE), 0)
                    == buckets_ref[r, t : t + 1, cols]
                ).astype(f32).astype(bf16)
                product = (
                    jnp.dot(pos_lhs[...], chosen, preferred_element_type=f32) * keys_t[:, cols]
                )
                heads_sum = jnp.sum(product.reshape(HEADS, HEAD_DIM, TILE), axis=1)
                for sub in range(TILE // LANES):
                    at = (half * (TILE // LANES) + sub) * table_rows + t * HEADS
                    from_pos[r, at : at + HEADS, :] = heads_sum[
                        :, sub * LANES : (sub + 1) * LANES
                    ]
        return carry

    lax.fori_loop(0, GROUP, from_pos_step, 0)

    first = me * PIECE

    def message_copies(r, k):
        peer = (r // 2) * SIDE + k
        slot = lax.rem(peer - me + SEQ_N, SEQ_N) - 1
        part = lax.rem(r, 2)
        return peer, [
            near_copy(msg_numer.at[r], in_numer.at[slot, part], n_send, n_recv, "seq", peer),
            near_copy(msg_ml.at[r], in_ml.at[slot, part], m_send, m_recv, "seq", peer),
        ]

    def attend_step(step, carry):
        r = 2 * x_slot(step // 2 + 1) + lax.rem(step, 2)

        @pl.when(step == FORWARD)
        def _():
            wait_all(far_copies())
            start_all(forward_copies((2,)))

        value_copy(r).wait()
        span = pl.ds(pl.multiple_of(r * table_rows, table_rows), table_rows)
        content = dot_nt(queries[span, :], keys[r])
        parts = []
        for t in range(NEW):
            tables = [
                q_table[
                    pl.ds(pl.multiple_of(r * table_rows + t * HEADS, HEADS), HEADS),
                    kb * LANES : (kb + 1) * LANES,
                ]
                for kb in range(BUCKETS // LANES)
            ]
            columns = []
            for sub in range(PIECE // LANES):
                bucket = jnp.broadcast_to(
                    buckets_ref[r, t : t + 1, sub * LANES : (sub + 1) * LANES], (HEADS, LANES)
                )
                low = bucket & (LANES - 1)
                high = bucket >> 7
                picked = jnp.take_along_axis(tables[0], low, axis=1)
                for kb in range(1, BUCKETS // LANES):
                    picked = jnp.where(
                        high == kb, jnp.take_along_axis(tables[kb], low, axis=1), picked
                    )
                back = jnp.concatenate(
                    [
                        from_pos[
                            r, pl.ds(sub * table_rows + t * HEADS + j, CHUNKS, stride=2), :
                        ]
                        for j in range(2)
                    ],
                    axis=0,
                )
                columns.append(picked + back)
            parts.append(jnp.concatenate(columns, axis=1))
        total = content + jnp.concatenate(parts, axis=0)
        position = first + lax.broadcasted_iota(jnp.int32, (table_rows, PIECE), 1)
        allowed = (position < lengths_ref[r]) & (
            (position < SINKS) | (position >= starts_ref[r])
        )
        scores = jnp.where(allowed, total * score_scale, masked_score)
        top = jnp.max(scores, axis=1, keepdims=True)
        weights = jnp.where(allowed, jnp.exp(scores - top), 0.0)
        sums = jnp.sum(weights, axis=1, keepdims=True)
        wide = jnp.dot(weights.astype(bf16), values[r], preferred_element_type=f32)
        numer = jnp.sum(jnp.where(own_head(), wide.reshape(NEW, HEADS, WIDTH), 0.0), axis=1)
        rows_to_tiles(numer, v_stage, NEW)
        msg_numer[r] = v_stage[0 : NEW * CHUNKS, :].astype(bf16)
        columns = []
        for token in range(NEW):
            for j in range(2):
                at = token * HEADS + j * CHUNKS
                columns.append(top[at : at + CHUNKS])
                columns.append(sums[at : at + CHUNKS])
        msg_ml[r] = pack_ml(columns, lane)
        for k in range(SIDE):
            peer, copies = message_copies(r, k)

            @pl.when(peer != me)
            def _():
                start_all(copies)

        return carry

    lax.fori_loop(0, GROUP, attend_step, 0)

    new_lane = lax.broadcasted_iota(jnp.int32, (NEW, NEW, GROUP), 2)
    new_all = new_ref[...].astype(f32)
    for i in range(2):
        wanted = jnp.sum(
            jnp.where(new_lane == 2 * at_x + i, new_all, 0.0), axis=2, keepdims=True
        )
        for t in range(NEW):
            at = (i * NEW + t) * NEW
            picks[at : at + NEW, :] = wanted[t]
    picked = (
        lax.broadcasted_iota(jnp.int32, (2 * NEW * NEW, BUCKETS), 1).astype(f32) == picks[...]
    ).astype(f32).astype(bf16)
    pq = dot_nt(picked, pos_lhs[...])
    pk = jnp.dot(picked, pos_key[...], preferred_element_type=f32)
    for i in range(2):
        mine = proj[2 * at_x + i]
        q4, k4, v4 = (mine[:, w * WIDTH : (w + 1) * WIDTH] for w in range(3))
        pairs = NEW * NEW
        q16 = jnp.broadcast_to(q4[:, None, :], (NEW, NEW, WIDTH)).reshape(pairs, WIDTH)
        k16 = jnp.broadcast_to(k4[None], (NEW, NEW, WIDTH)).reshape(pairs, WIDTH)
        span = slice(i * pairs, (i + 1) * pairs)
        rows_to_tiles(q16 * (k16 + pk[span]) + k16 * pq[span], fresh_stage, pairs)
        rows_to_tiles(v4, v_stage, NEW)
        columns = []
        for t in range(NEW):
            spread = []
            for u in range(t + 1):
                at = (t * NEW + u) * CHUNKS
                terms = fresh_stage[at : at + CHUNKS, :]
                even = jnp.sum(jnp.where(lane < HEAD_DIM, terms, 0.0), axis=1, keepdims=True)
                other = jnp.sum(jnp.where(lane >= HEAD_DIM, terms, 0.0), axis=1, keepdims=True)
                spread.append(spread_pair(even, other, lane) * score_scale)
            top = functools.reduce(jnp.maximum, spread)
            sums = jnp.zeros_like(top)
            numer = jnp.zeros_like(top)
            for u in range(t + 1):
                weight = jnp.exp(spread[u] - top)
                sums = sums + weight
                numer = numer + weight.astype(bf16).astype(f32) * v_stage[
                    u * CHUNKS : (u + 1) * CHUNKS, :
                ]
            fresh_numer[i, t * CHUNKS : (t + 1) * CHUNKS, :] = numer
            for at in (0, HEAD_DIM):
                columns.append(top[:, at : at + 1])
                columns.append(sums[:, at : at + 1])
        fresh_ml[i] = pack_ml(columns, lane)

    near_copy(in_numer, in_numer, n_send, n_recv, "seq", x_peer(1)).wait()
    near_copy(in_ml, in_ml, m_send, m_recv, "seq", x_peer(1)).wait()
    for i in range(2):
        mls = [in_ml[k, i] for k in range(SEQ_N - 1)] + [msg_ml[2 * at_x + i], fresh_ml[i]]
        top = functools.reduce(jnp.maximum, mls)
        factors = [jnp.exp(ml - top) for ml in mls]
        denom = functools.reduce(
            jnp.add, [f * pltpu.roll(ml, LANES - 8, axis=1) for f, ml in zip(factors, mls)]
        )
        numers = [jnp.zeros((CHUNKS, LANES), f32) for _ in range(NEW)]
        for k, factor in enumerate(factors):
            if k < SEQ_N - 1:
                block = in_numer[k, i].astype(f32)
            elif k == SEQ_N - 1:
                block = msg_numer[2 * at_x + i].astype(f32)
            else:
                block = fresh_numer[i]
            for t in range(NEW):
                at = t * 32
                numers[t] = numers[t] + block[t * CHUNKS : (t + 1) * CHUNKS] * spread_pair(
                    factor[:, at : at + 1], factor[:, at + 16 : at + 17], lane
                )
        for t in range(NEW):
            at = t * 32
            row = (i * NEW + t) * CHUNKS
            att[row : row + CHUNKS, :] = numers[t] / spread_pair(
                denom[:, at : at + 1], denom[:, at + 16 : at + 17], lane
            )
    attended = tiles_to_rows(att, 2 * NEW).astype(bf16)
    out_copy.wait()
    attn_out = jnp.dot(attended, w_out[...], preferred_element_type=f32)
    hidden_one = layer_norm(
        h_zero[at_x] + attn_out, gain_ref[1:2, :], bias_ref[1:2, :]
    ).astype(bf16)
    wait_all(forward_copies((1, 2, 3)))
    total = jnp.zeros((2 * NEW, WIDTH), f32)
    for one in range(SIDE):
        inner = dot_nt(hidden_one, w_ff[0, one])
        inner = (0.5 * inner * (1.0 + lax.erf(inner * math.sqrt(0.5)))).astype(bf16)
        total = total + jnp.dot(inner, w_ff[1, one], preferred_element_type=f32)
    partial[at_y] = total.astype(bf16)
    copies = [
        near_copy(
            partial.at[at_y], partial.at[at_y], y_send.at[k], y_recv.at[k], "seq", y_peer(k)
        )
        for k in range(1, SIDE)
    ]
    start_all(copies)
    wait_all(copies)
    mlp_out = functools.reduce(jnp.add, [partial[k].astype(f32) for k in range(SIDE)])
    final[at_x] = layer_norm(
        hidden_one.astype(f32) + mlp_out, gain_ref[2:3, :], bias_ref[2:3, :]
    ).astype(bf16)
    copies = [
        near_copy(final.at[at_x], final.at[at_x], x_send.at[k], x_recv.at[k], "seq", x_peer(k))
        for k in range(1, SIDE)
    ]
    start_all(copies)
    wait_all(copies)
    for one in range(SIDE):
        rows = final[one].astype(f32)
        for i in range(2):
            out_ref[2 * one + i] = rows[i * NEW : (i + 1) * NEW, :].astype(bf16)


def shards(
    token_ids,
    embed_table,
    ln_gains,
    ln_biases,
    rel_table,
    w_qkv,
    w_out,
    cache_keys,
    cache_values,
    lengths,
    window_starts,
    cache_buckets,
    new_buckets,
    w_in,
    w_down,
):
    slot = (SEQ_N, 2 * CHUNKS, LANES)
    in_vmem = pl.BlockSpec(memory_space=pltpu.VMEM)
    in_smem = pl.BlockSpec(memory_space=pltpu.SMEM)
    in_place = pl.BlockSpec(memory_space=pl.ANY)
    return pl.pallas_call(
        layer_kernel,
        out_shape=jax.ShapeDtypeStruct((GROUP, NEW, WIDTH), bf16),
        in_specs=[
            in_vmem, in_place, in_vmem, in_vmem, in_place, in_place, in_place, in_place, in_place,
            in_smem, in_smem, in_vmem, in_vmem, in_place, in_place,
        ],
        out_specs=in_vmem,
        scratch_shapes=[
            pltpu.VMEM(embed_table.shape, bf16),
            pltpu.VMEM(rel_table.shape, bf16),
            pltpu.VMEM(w_qkv.shape, bf16),
            pltpu.VMEM(w_out.shape, bf16),
            pltpu.VMEM(cache_keys.shape, bf16),
            pltpu.VMEM(cache_values.shape, bf16),
            pltpu.VMEM((2, SIDE) + w_in.shape, bf16),
            pltpu.VMEM((8, LANES), jnp.int32),
            pltpu.VMEM((REQ_N, ROWS, WIDTH), bf16),
            pltpu.VMEM((REQ_N, ROWS, WIDTH), bf16),
            pltpu.VMEM((ROWS * CHUNKS, LANES), f32),
            pltpu.VMEM((1,) + slot, bf16),
            pltpu.VMEM((1,) + slot, bf16),
            pltpu.VMEM((1,) + slot, bf16),
            pltpu.VMEM((SIDE, 2 * NEW, WIDTH), f32),
            pltpu.VMEM((2 * CHUNKS, LANES), f32),
            pltpu.VMEM((2 * NEW * CHUNKS, LANES), f32),
            pltpu.VMEM((GROUP, NEW, 3 * WIDTH), f32),
            pltpu.VMEM((WIDTH, BUCKETS), bf16),
            pltpu.VMEM((BUCKETS, WIDTH), bf16),
            pltpu.VMEM((WIDTH, PIECE), f32),
            pltpu.VMEM((GROUP, PIECE // LANES * NEW * HEADS, LANES), f32),
            pltpu.VMEM((GROUP * NEW * HEADS, WIDTH), bf16),
            pltpu.VMEM((GROUP * NEW * HEADS, BUCKETS), f32),
            pltpu.VMEM((GROUP, NEW * CHUNKS, LANES), bf16),
            pltpu.VMEM((GROUP, CHUNKS, LANES), f32),
            pltpu.VMEM((SEQ_N - 1, 2, NEW * CHUNKS, LANES), bf16),
            pltpu.VMEM((SEQ_N - 1, 2, CHUNKS, LANES), f32),
            pltpu.VMEM((2, NEW * CHUNKS, LANES), f32),
            pltpu.VMEM((2, CHUNKS, LANES), f32),
            pltpu.VMEM((NEW * NEW * CHUNKS, LANES), f32),
            pltpu.VMEM((NEW * CHUNKS, LANES), f32),
            pltpu.VMEM((2 * NEW * NEW, 1), f32),
            pltpu.VMEM((SIDE, 2 * NEW, WIDTH), bf16),
            pltpu.VMEM((SIDE, 2 * NEW, WIDTH), bf16),
            pltpu.SemaphoreType.DMA((8,)),
            pltpu.SemaphoreType.DMA((GROUP,)),
            pltpu.SemaphoreType.DMA((GROUP,)),
        ]
        + [pltpu.SemaphoreType.DMA((REQ_N,))] * 2
        + [pltpu.SemaphoreType.DMA((SEQ_N,))] * 4
        + [pltpu.SemaphoreType.DMA] * 4
        + [pltpu.SemaphoreType.DMA((SIDE,))] * 8,
        compiler_params=pltpu.CompilerParams(
            collective_id=0, has_side_effects=True, vmem_limit_bytes=60 << 20
        ),
        name="decode_layer",
    )(
        token_ids.T, embed_table, ln_gains, ln_biases, rel_table, w_qkv, w_out, cache_keys,
        cache_values, lengths, window_starts, cache_buckets,
        jnp.transpose(new_buckets, (1, 2, 0)), w_in, w_down,
    )


def solution(mesh):
    in_specs = (
        P(),
        P(("req", "seq"), None),
        P(),
        P(),
        P(),
        P(),
        P(),
        P("req", "seq", None),
        P("req", "seq", None),
        P("req"),
        P("req"),
        P("req", None, "seq"),
        P("req", None, None),
        P("seq", None),
        P("seq", None),
    )
    out_specs = P("req", None, None)
    return jax.shard_map(shards, mesh=mesh, in_specs=in_specs, out_specs=out_specs, check_vma=False)
```

```python
import functools
import math

import jax
import jax.numpy as jnp
from jax import lax
from jax.experimental import pallas as pl
from jax.experimental.pallas import tpu as pltpu
from jax.sharding import PartitionSpec as P

HEADS = 16
HEAD_DIM = 64
SINKS = 4
NEW = 4
WIDTH = 1024
REQ_N = 8
SEQ_N = 16
GROUP = 8
ROWS = GROUP * NEW
PIECE = 512
BUCKETS = 512
TILE = 256
LANES = 128
CHUNKS = WIDTH // LANES
SIDE = 4
HOOKS = (3, 5, 7)
PASS_ON = 6
FORWARD = 6

norm_epsilon = 1e-06
masked_score = -1e30
score_scale = 1.0 / math.sqrt(3 * HEAD_DIM)
MESH = pl.DeviceIdType.MESH
f32 = jnp.float32
bf16 = jnp.bfloat16


def layer_norm(values, gain, shift):
    center = values - jnp.mean(values, axis=-1, keepdims=True)
    spread = jnp.mean(center * center, axis=-1, keepdims=True)
    return center * lax.rsqrt(spread + norm_epsilon) * gain + shift


def dot_nt(a, b):
    return lax.dot_general(a, b, (((1,), (1,)), ((), ())), preferred_element_type=f32)


def rows_to_tiles(rows, stage, count):
    for c in range(CHUNKS):
        stage[pl.ds(c, count, stride=CHUNKS), :] = rows[:, c * LANES : (c + 1) * LANES]


def tiles_to_rows(stage, count):
    return jnp.concatenate(
        [stage[pl.ds(c, count, stride=CHUNKS), :] for c in range(CHUNKS)], axis=1
    )


def seq_copy(src, dst, send_sem, recv_sem, peer):
    return pltpu.make_async_remote_copy(
        src_ref=src,
        dst_ref=dst,
        send_sem=send_sem,
        recv_sem=recv_sem,
        device_id={"seq": peer},
        device_id_type=MESH,
    )


def seq_scatter(me, send, recv, send_sems, recv_sems):
    copies = []
    for k in range(1, SEQ_N):
        peer = lax.rem(me + k, SEQ_N)
        copy = seq_copy(send.at[peer], recv.at[k], send_sems.at[k], recv_sems.at[k], peer)
        copies.append(copy)
    return copies


def seq_gather(me, buf, send_sems, recv_sems):
    copies = []
    for k in range(1, SEQ_N):
        peer = lax.rem(me + k, SEQ_N)
        copy = seq_copy(buf.at[me], buf.at[me], send_sems.at[k], recv_sems.at[k], peer)
        copies.append(copy)
    return copies


def start_all(copies):
    for copy in copies:
        copy.start()


def wait_all(copies):
    for copy in copies:
        copy.wait()


def spread_pair(column_even, column_odd, lane):
    return jnp.where(lane < HEAD_DIM, column_even, column_odd)


def pack_ml(values, lane):
    out = jnp.zeros((CHUNKS, LANES), f32)
    for g, value in enumerate(values):
        out = jnp.where((lane >> 3) == g, value, out)
    return out


def layer_kernel(
    ids_ref, table_hbm, gain_ref, bias_ref, rel_hbm, w_hbm, w_out_hbm, keys_hbm, values_hbm,
    lengths_ref, starts_ref, buckets_ref, new_ref, w_in_hbm, w_down_hbm,
    out_ref,
    table, rel, w_qkv, w_out, keys, values, w_ff, ids_pad,
    send, land, stage, tiles, got, hid, h_zero, rows_f, att, proj, pos_lhs, pos_key, keys_t,
    from_pos, queries, q_table, msg_numer, msg_ml, in_numer, in_ml, fresh_numer, fresh_ml,
    fresh_stage, v_stage, picks, partial, final,
    local_sems, key_sems, value_sems,
    req_send, req_recv, rs_send, rs_recv, ag_send, ag_recv,
    n_send, n_recv, m_send, m_recv, w_send, w_recv, f_send, f_recv, y_send, y_recv, x_send, x_recv,
):
    me = lax.axis_index("seq")
    req = lax.axis_index("req")
    at_x, at_y = me // SIDE, lax.rem(me, SIDE)
    core = lax.rem(req, 2)
    table_rows = NEW * HEADS
    lane = lax.broadcasted_iota(jnp.int32, (CHUNKS, LANES), 1)

    def local(src, dst, index):
        return pltpu.make_async_copy(src, dst, local_sems.at[index])

    table_copy = local(table_hbm, table, 0)
    rel_copy = local(rel_hbm, rel, 1)
    w_copies = [
        local(
            w_hbm.at[:, i * WIDTH : (i + 1) * WIDTH], w_qkv.at[:, i * WIDTH : (i + 1) * WIDTH], 2 + i
        )
        for i in range(3)
    ]
    out_copy = local(w_out_hbm, w_out, 5)
    in_copy = local(w_in_hbm, w_ff.at[0, at_x], 6)
    down_copy = local(w_down_hbm, w_ff.at[1, at_x], 7)

    def key_copy(r):
        return pltpu.make_async_copy(keys_hbm.at[r], keys.at[r], key_sems.at[r])

    def value_copy(r):
        return pltpu.make_async_copy(values_hbm.at[r], values.at[r], value_sems.at[r])

    in_copy.start()
    down_copy.start()
    table_copy.start()
    rel_copy.start()
    w_copies[0].start()
    w_copies[1].start()
    barrier = pltpu.get_barrier_semaphore()
    for k in range(1, SEQ_N):
        pl.semaphore_signal(
            barrier, inc=1, device_id={"seq": lax.rem(me + k, SEQ_N)}, device_id_type=MESH
        )
    for k in range(1, REQ_N):
        pl.semaphore_signal(
            barrier, inc=1, device_id={"req": lax.rem(req + k, REQ_N)}, device_id_type=MESH
        )
    key_copy(0).start()

    vocab_rows = table.shape[0]
    ids_pad[...] = jnp.zeros((8, LANES), jnp.int32)
    ids_pad[0:NEW, 0 : REQ_N * GROUP] = ids_ref[...]
    ids_t = ids_pad[...].T
    ids = jnp.concatenate(
        [
            ids_t[g * GROUP : (g + 1) * GROUP, t : t + 1]
            for g in range(REQ_N)
            for t in range(NEW)
        ],
        axis=0,
    ) - (req * SEQ_N + me) * vocab_rows
    one_hot = (
        lax.broadcasted_iota(jnp.int32, (REQ_N * ROWS, vocab_rows), 1) == ids
    ).astype(f32).astype(bf16)
    table_copy.wait()
    send[...] = (
        jnp.dot(one_hot, table[...], preferred_element_type=f32)
        .astype(bf16)
        .reshape(REQ_N, ROWS, WIDTH)
    )
    rel_copy.wait()
    relative = layer_norm(rel[...].astype(f32), gain_ref[3:4, :], bias_ref[3:4, :]).astype(bf16)
    pl.semaphore_wait(barrier, SEQ_N - 1 + REQ_N - 1)

    def req_copies():
        copies = []
        for k in range(1, REQ_N):
            peer = lax.rem(req + k, REQ_N)
            copies.append(
                pltpu.make_async_remote_copy(
                    src_ref=send.at[peer],
                    dst_ref=land.at[k],
                    send_sem=req_send.at[k],
                    recv_sem=req_recv.at[k],
                    device_id={"req": peer},
                    device_id_type=MESH,
                )
            )
        return copies

    for copy in req_copies():
        copy.start()

    def near_copy(src, dst, send_sem, recv_sem, axis, peer):
        return pltpu.make_async_remote_copy(
            src_ref=src,
            dst_ref=dst,
            send_sem=send_sem,
            recv_sem=recv_sem,
            device_id={axis: peer},
            device_id_type=MESH,
        )

    def x_slot(k):
        return lax.rem(at_x + k, SIDE)

    def x_peer(k):
        return x_slot(k) * SIDE + at_y

    def y_peer(k):
        return at_x * SIDE + lax.rem(at_y + k, SIDE)

    def shard_copies():
        held = w_ff.at[core, at_x]
        return [
            near_copy(held, held, w_send.at[k], w_recv.at[k], "seq", x_peer(k)) for k in (1, 3)
        ]

    def far_copies():
        half = w_ff.shape[2] // 2
        copies = []
        for index, (k, rows) in enumerate(((1, slice(0, half)), (3, slice(half, 2 * half)))):
            held = w_ff.at[core, x_slot(k + 2), rows]
            copies.append(
                near_copy(held, held, w_send.at[2 * index], w_recv.at[2 * index], "seq", x_peer(k))
            )
        return copies

    def forward_copies(offsets):
        copies = []
        for k in offsets:
            held = w_ff.at[core, x_slot(k)]
            copies.append(
                near_copy(held, held, f_send.at[k], f_recv.at[k], "req", req + 1 - 2 * core)
            )
        return copies

    in_copy.wait()
    down_copy.wait()
    start_all(shard_copies())

    w_copies[0].wait()
    pos_lhs[...] = (
        jnp.dot(relative, w_qkv[:, 0:WIDTH], preferred_element_type=f32).astype(bf16).T
    )
    w_copies[1].wait()
    key_copy(1).start()
    w_copies[2].start()
    pos_key[...] = jnp.dot(
        relative, w_qkv[:, WIDTH : 2 * WIDTH], preferred_element_type=f32
    ).astype(bf16)

    def own_head():
        row = lax.broadcasted_iota(jnp.int32, (NEW, HEADS, WIDTH), 1)
        col_head = lax.broadcasted_iota(jnp.int32, (NEW, HEADS, WIDTH), 2) >> 6
        return 2 * (row & (CHUNKS - 1)) + (row >> 3) == col_head

    def from_pos_step(r, carry):
        value_copy(r).start()

        @pl.when(r < GROUP - 2)
        def _():
            key_copy(r + 2).start()

        @pl.when(r == 0)
        def _():
            out_copy.start()

        @pl.when(r == PASS_ON)
        def _():
            wait_all(shard_copies())
            start_all(far_copies())
            start_all(forward_copies((1, 3)))

        @pl.when(r == HOOKS[0])
        def _():
            copies = req_copies()
            total = send[req].astype(f32)
            for k in range(1, REQ_N):
                copies[k - 1].wait()
                total = total + land[k].astype(f32)
            for t in range(NEW):
                for c in range(CHUNKS):
                    stage[pl.ds(t * CHUNKS + c, GROUP, stride=NEW * CHUNKS), :] = total[
                        t * GROUP : (t + 1) * GROUP, c * LANES : (c + 1) * LANES
                    ]
            tiles[0] = stage[...].reshape(SEQ_N, 2 * CHUNKS, LANES).astype(bf16)
            start_all(seq_scatter(me, tiles.at[0], got.at[0], rs_send, rs_recv))

        @pl.when(r == HOOKS[1])
        def _():
            copies = seq_scatter(me, tiles.at[0], got.at[0], rs_send, rs_recv)
            own = tiles[0, me].astype(f32)
            for k in range(1, SEQ_N):
                copies[k - 1].wait()
                own = own + got[0, k].astype(f32)
            rows_f[...] = own
            hidden = layer_norm(tiles_to_rows(rows_f, 2), gain_ref[0:1, :], bias_ref[0:1, :])
            rows_to_tiles(hidden, rows_f, 2)
            hid[0, me] = rows_f[...].astype(bf16)
            start_all(seq_gather(me, hid.at[0], ag_send, ag_recv))

        @pl.when(r == HOOKS[2])
        def _():
            wait_all(seq_gather(me, hid.at[0], ag_send, ag_recv))
            stage[...] = hid[0].astype(f32).reshape(ROWS * CHUNKS, LANES)
            hidden = tiles_to_rows(stage, ROWS)
            for one in range(SIDE):
                h_zero[one] = hidden[one * 2 * NEW : (one + 1) * 2 * NEW, :]
            hidden = hidden.astype(bf16)
            w_copies[2].wait()
            projected = (
                jnp.dot(hidden, w_qkv[...], preferred_element_type=f32).astype(bf16).astype(f32)
            )
            mine = own_head()
            for one in range(GROUP):
                block = projected[one * NEW : (one + 1) * NEW, :]
                proj[one] = block
                q_all = jnp.broadcast_to(block[:, None, 0:WIDTH], (NEW, HEADS, WIDTH))
                queries[one * table_rows : (one + 1) * table_rows, :] = (
                    jnp.where(mine, q_all, 0.0).reshape(table_rows, WIDTH).astype(bf16)
                )
            q_table[...] = dot_nt(queries[...], pos_key[...])

        key_copy(r).wait()
        keys_t[...] = keys[r].T.astype(f32)
        for t in range(NEW):
            for half in range(PIECE // TILE):
                cols = slice(half * TILE, (half + 1) * TILE)
                chosen = (
                    lax.broadcasted_iota(jnp.int32, (BUCKETS, TILE), 0)
                    == BUCKETS - 1 - buckets_ref[r, t : t + 1, cols]
                ).astype(f32).astype(bf16)
                product = (
                    jnp.dot(pos_lhs[...], chosen, preferred_element_type=f32) * keys_t[:, cols]
                )
                heads_sum = jnp.sum(product.reshape(HEADS, HEAD_DIM, TILE), axis=1)
                for sub in range(TILE // LANES):
                    at = (half * (TILE // LANES) + sub) * table_rows + t * HEADS
                    from_pos[r, at : at + HEADS, :] = heads_sum[
                        :, sub * LANES : (sub + 1) * LANES
                    ]
        return carry

    lax.fori_loop(0, GROUP, from_pos_step, 0)

    first = me * PIECE

    def message_copies(r, k):
        peer = (r // 2) * SIDE + k
        slot = lax.rem(peer - me + SEQ_N, SEQ_N) - 1
        part = lax.rem(r, 2)
        return peer, [
            near_copy(msg_numer.at[r], in_numer.at[slot, part], n_send, n_recv, "seq", peer),
            near_copy(msg_ml.at[r], in_ml.at[slot, part], m_send, m_recv, "seq", peer),
        ]

    def attend_step(step, carry):
        r = 2 * x_slot(step // 2 + 1) + lax.rem(step, 2)

        @pl.when(step == FORWARD)
        def _():
            wait_all(far_copies())
            start_all(forward_copies((2,)))

        value_copy(r).wait()
        span = pl.ds(pl.multiple_of(r * table_rows, table_rows), table_rows)
        content = dot_nt(queries[span, :], keys[r])
        parts = []
        for t in range(NEW):
            tables = [
                q_table[
                    pl.ds(pl.multiple_of(r * table_rows + t * HEADS, HEADS), HEADS),
                    kb * LANES : (kb + 1) * LANES,
                ]
                for kb in range(BUCKETS // LANES)
            ]
            columns = []
            for sub in range(PIECE // LANES):
                bucket = jnp.broadcast_to(
                    buckets_ref[r, t : t + 1, sub * LANES : (sub + 1) * LANES], (HEADS, LANES)
                )
                low = bucket & (LANES - 1)
                high = bucket >> 7
                picked = jnp.take_along_axis(tables[0], low, axis=1)
                for kb in range(1, BUCKETS // LANES):
                    picked = jnp.where(
                        high == kb, jnp.take_along_axis(tables[kb], low, axis=1), picked
                    )
                back = jnp.concatenate(
                    [
                        from_pos[
                            r, pl.ds(sub * table_rows + t * HEADS + j, CHUNKS, stride=2), :
                        ]
                        for j in range(2)
                    ],
                    axis=0,
                )
                columns.append(picked + back)
            parts.append(jnp.concatenate(columns, axis=1))
        total = content + jnp.concatenate(parts, axis=0)
        position = first + lax.broadcasted_iota(jnp.int32, (table_rows, PIECE), 1)
        allowed = (position < lengths_ref[r]) & (
            (position < SINKS) | (position >= starts_ref[r])
        )
        scores = jnp.where(allowed, total * score_scale, masked_score)
        top = jnp.max(scores, axis=1, keepdims=True)
        weights = jnp.where(allowed, jnp.exp(scores - top), 0.0)
        sums = jnp.sum(weights, axis=1, keepdims=True)
        wide = jnp.dot(weights.astype(bf16), values[r], preferred_element_type=f32)
        numer = jnp.sum(jnp.where(own_head(), wide.reshape(NEW, HEADS, WIDTH), 0.0), axis=1)
        rows_to_tiles(numer, v_stage, NEW)
        msg_numer[r] = v_stage[0 : NEW * CHUNKS, :].astype(bf16)
        columns = []
        for token in range(NEW):
            for j in range(2):
                at = token * HEADS + j * CHUNKS
                columns.append(top[at : at + CHUNKS])
                columns.append(sums[at : at + CHUNKS])
        msg_ml[r] = pack_ml(columns, lane)
        for k in range(SIDE):
            peer, copies = message_copies(r, k)

            @pl.when(peer != me)
            def _():
                start_all(copies)

        return carry

    lax.fori_loop(0, GROUP, attend_step, 0)

    new_lane = lax.broadcasted_iota(jnp.int32, (NEW, NEW, GROUP), 2)
    new_all = new_ref[...].astype(f32)
    for i in range(2):
        wanted = jnp.sum(
            jnp.where(new_lane == 2 * at_x + i, new_all, 0.0), axis=2, keepdims=True
        )
        for t in range(NEW):
            at = (i * NEW + t) * NEW
            picks[at : at + NEW, :] = wanted[t]
    buckets = lax.broadcasted_iota(jnp.int32, (2 * NEW * NEW, BUCKETS), 1).astype(f32)
    picked = (buckets == picks[...]).astype(f32).astype(bf16)
    mirrored = (buckets == BUCKETS - 1 - picks[...]).astype(f32).astype(bf16)
    pq = dot_nt(mirrored, pos_lhs[...])
    pk = jnp.dot(picked, pos_key[...], preferred_element_type=f32)
    for i in range(2):
        mine = proj[2 * at_x + i]
        q4, k4, v4 = (mine[:, w * WIDTH : (w + 1) * WIDTH] for w in range(3))
        pairs = NEW * NEW
        q16 = jnp.broadcast_to(q4[:, None, :], (NEW, NEW, WIDTH)).reshape(pairs, WIDTH)
        k16 = jnp.broadcast_to(k4[None], (NEW, NEW, WIDTH)).reshape(pairs, WIDTH)
        span = slice(i * pairs, (i + 1) * pairs)
        rows_to_tiles(q16 * (k16 + pk[span]) + k16 * pq[span], fresh_stage, pairs)
        rows_to_tiles(v4, v_stage, NEW)
        columns = []
        for t in range(NEW):
            spread = []
            for u in range(t + 1):
                at = (t * NEW + u) * CHUNKS
                terms = fresh_stage[at : at + CHUNKS, :]
                even = jnp.sum(jnp.where(lane < HEAD_DIM, terms, 0.0), axis=1, keepdims=True)
                other = jnp.sum(jnp.where(lane >= HEAD_DIM, terms, 0.0), axis=1, keepdims=True)
                spread.append(spread_pair(even, other, lane) * score_scale)
            top = functools.reduce(jnp.maximum, spread)
            sums = jnp.zeros_like(top)
            numer = jnp.zeros_like(top)
            for u in range(t + 1):
                weight = jnp.exp(spread[u] - top)
                sums = sums + weight
                numer = numer + weight.astype(bf16).astype(f32) * v_stage[
                    u * CHUNKS : (u + 1) * CHUNKS, :
                ]
            fresh_numer[i, t * CHUNKS : (t + 1) * CHUNKS, :] = numer
            for at in (0, HEAD_DIM):
                columns.append(top[:, at : at + 1])
                columns.append(sums[:, at : at + 1])
        fresh_ml[i] = pack_ml(columns, lane)

    near_copy(in_numer, in_numer, n_send, n_recv, "seq", x_peer(1)).wait()
    near_copy(in_ml, in_ml, m_send, m_recv, "seq", x_peer(1)).wait()
    for i in range(2):
        mls = [in_ml[k, i] for k in range(SEQ_N - 1)] + [msg_ml[2 * at_x + i], fresh_ml[i]]
        top = functools.reduce(jnp.maximum, mls)
        factors = [jnp.exp(ml - top) for ml in mls]
        denom = functools.reduce(
            jnp.add, [f * pltpu.roll(ml, LANES - 8, axis=1) for f, ml in zip(factors, mls)]
        )
        numers = [jnp.zeros((CHUNKS, LANES), f32) for _ in range(NEW)]
        for k, factor in enumerate(factors):
            if k < SEQ_N - 1:
                block = in_numer[k, i].astype(f32)
            elif k == SEQ_N - 1:
                block = msg_numer[2 * at_x + i].astype(f32)
            else:
                block = fresh_numer[i]
            for t in range(NEW):
                at = t * 32
                numers[t] = numers[t] + block[t * CHUNKS : (t + 1) * CHUNKS] * spread_pair(
                    factor[:, at : at + 1], factor[:, at + 16 : at + 17], lane
                )
        for t in range(NEW):
            at = t * 32
            row = (i * NEW + t) * CHUNKS
            att[row : row + CHUNKS, :] = numers[t] / spread_pair(
                denom[:, at : at + 1], denom[:, at + 16 : at + 17], lane
            )
    attended = tiles_to_rows(att, 2 * NEW).astype(bf16)
    out_copy.wait()
    attn_out = jnp.dot(attended, w_out[...], preferred_element_type=f32)
    hidden_one = layer_norm(
        h_zero[at_x] + attn_out, gain_ref[1:2, :], bias_ref[1:2, :]
    ).astype(bf16)
    wait_all(forward_copies((1, 2, 3)))
    total = jnp.zeros((2 * NEW, WIDTH), f32)
    for one in range(SIDE):
        inner = dot_nt(hidden_one, w_ff[0, one])
        inner = (0.5 * inner * (1.0 + lax.erf(inner * math.sqrt(0.5)))).astype(bf16)
        total = total + jnp.dot(inner, w_ff[1, one], preferred_element_type=f32)
    partial[at_y] = total.astype(bf16)
    copies = [
        near_copy(
            partial.at[at_y], partial.at[at_y], y_send.at[k], y_recv.at[k], "seq", y_peer(k)
        )
        for k in range(1, SIDE)
    ]
    start_all(copies)
    wait_all(copies)
    mlp_out = functools.reduce(jnp.add, [partial[k].astype(f32) for k in range(SIDE)])
    final[at_x] = layer_norm(
        hidden_one.astype(f32) + mlp_out, gain_ref[2:3, :], bias_ref[2:3, :]
    ).astype(bf16)
    copies = [
        near_copy(final.at[at_x], final.at[at_x], x_send.at[k], x_recv.at[k], "seq", x_peer(k))
        for k in range(1, SIDE)
    ]
    start_all(copies)
    wait_all(copies)
    for one in range(SIDE):
        rows = final[one].astype(f32)
        for i in range(2):
            out_ref[2 * one + i] = rows[i * NEW : (i + 1) * NEW, :].astype(bf16)


def shards(
    token_ids,
    embed_table,
    ln_gains,
    ln_biases,
    rel_table,
    w_qkv,
    w_out,
    cache_keys,
    cache_values,
    lengths,
    window_starts,
    cache_buckets,
    new_buckets,
    w_in,
    w_down,
):
    slot = (SEQ_N, 2 * CHUNKS, LANES)
    in_vmem = pl.BlockSpec(memory_space=pltpu.VMEM)
    in_smem = pl.BlockSpec(memory_space=pltpu.SMEM)
    in_place = pl.BlockSpec(memory_space=pl.ANY)
    return pl.pallas_call(
        layer_kernel,
        out_shape=jax.ShapeDtypeStruct((GROUP, NEW, WIDTH), bf16),
        in_specs=[
            in_vmem, in_place, in_vmem, in_vmem, in_place, in_place, in_place, in_place, in_place,
            in_smem, in_smem, in_vmem, in_vmem, in_place, in_place,
        ],
        out_specs=in_vmem,
        scratch_shapes=[
            pltpu.VMEM(embed_table.shape, bf16),
            pltpu.VMEM(rel_table.shape, bf16),
            pltpu.VMEM(w_qkv.shape, bf16),
            pltpu.VMEM(w_out.shape, bf16),
            pltpu.VMEM(cache_keys.shape, bf16),
            pltpu.VMEM(cache_values.shape, bf16),
            pltpu.VMEM((2, SIDE) + w_in.shape, bf16),
            pltpu.VMEM((8, LANES), jnp.int32),
            pltpu.VMEM((REQ_N, ROWS, WIDTH), bf16),
            pltpu.VMEM((REQ_N, ROWS, WIDTH), bf16),
            pltpu.VMEM((ROWS * CHUNKS, LANES), f32),
            pltpu.VMEM((1,) + slot, bf16),
            pltpu.VMEM((1,) + slot, bf16),
            pltpu.VMEM((1,) + slot, bf16),
            pltpu.VMEM((SIDE, 2 * NEW, WIDTH), f32),
            pltpu.VMEM((2 * CHUNKS, LANES), f32),
            pltpu.VMEM((2 * NEW * CHUNKS, LANES), f32),
            pltpu.VMEM((GROUP, NEW, 3 * WIDTH), f32),
            pltpu.VMEM((WIDTH, BUCKETS), bf16),
            pltpu.VMEM((BUCKETS, WIDTH), bf16),
            pltpu.VMEM((WIDTH, PIECE), f32),
            pltpu.VMEM((GROUP, PIECE // LANES * NEW * HEADS, LANES), f32),
            pltpu.VMEM((GROUP * NEW * HEADS, WIDTH), bf16),
            pltpu.VMEM((GROUP * NEW * HEADS, BUCKETS), f32),
            pltpu.VMEM((GROUP, NEW * CHUNKS, LANES), bf16),
            pltpu.VMEM((GROUP, CHUNKS, LANES), f32),
            pltpu.VMEM((SEQ_N - 1, 2, NEW * CHUNKS, LANES), bf16),
            pltpu.VMEM((SEQ_N - 1, 2, CHUNKS, LANES), f32),
            pltpu.VMEM((2, NEW * CHUNKS, LANES), f32),
            pltpu.VMEM((2, CHUNKS, LANES), f32),
            pltpu.VMEM((NEW * NEW * CHUNKS, LANES), f32),
            pltpu.VMEM((NEW * CHUNKS, LANES), f32),
            pltpu.VMEM((2 * NEW * NEW, 1), f32),
            pltpu.VMEM((SIDE, 2 * NEW, WIDTH), bf16),
            pltpu.VMEM((SIDE, 2 * NEW, WIDTH), bf16),
            pltpu.SemaphoreType.DMA((8,)),
            pltpu.SemaphoreType.DMA((GROUP,)),
            pltpu.SemaphoreType.DMA((GROUP,)),
        ]
        + [pltpu.SemaphoreType.DMA((REQ_N,))] * 2
        + [pltpu.SemaphoreType.DMA((SEQ_N,))] * 4
        + [pltpu.SemaphoreType.DMA] * 4
        + [pltpu.SemaphoreType.DMA((SIDE,))] * 8,
        compiler_params=pltpu.CompilerParams(
            collective_id=0, has_side_effects=True, vmem_limit_bytes=60 << 20
        ),
        name="decode_layer",
    )(
        token_ids.T, embed_table, ln_gains, ln_biases, rel_table, w_qkv, w_out, cache_keys,
        cache_values, lengths, window_starts, cache_buckets,
        jnp.transpose(new_buckets, (1, 2, 0)), w_in, w_down,
    )


def solution(mesh):
    in_specs = (
        P(),
        P(("req", "seq"), None),
        P(),
        P(),
        P(),
        P(),
        P(),
        P("req", "seq", None),
        P("req", "seq", None),
        P("req"),
        P("req"),
        P("req", None, "seq"),
        P("req", None, None),
        P("seq", None),
        P("seq", None),
    )
    out_specs = P("req", None, None)
    return jax.shard_map(shards, mesh=mesh, in_specs=in_specs, out_specs=out_specs, check_vma=False)
```
